32 devices in a mesh: expert: 16 (over z, y, x), dp: 2 (over core).
Axes of the slice: x: 2, y: 2, z: 4, core: 2. Of those that a mesh axis runs over, the one named last changes fastest.
Arguments:
- pooled: bfloat16 [8192, 256], P(('expert', 'dp')), may hold values from -6 to 6
- routes: int32 [8192, 2], P(('expert', 'dp')), may hold values from 0 to 15, all different within a row; in each aligned block of 256 rows (0 to 255, 256 to 511, ...) at most 48 rows name the same one
- labels: int32 [8192, 2], P(('expert', 'dp')), may hold values from 0 to 1
- in_weight: bfloat16 [16, 4096, 256], P('expert'), may hold values from -0.375 to 0.375
- out_weight: bfloat16 [16, 4096, 256], P('expert'), may hold values from -0.09375 to 0.09375
- gate_weight: bfloat16 [16, 2, 256], replicated, may hold values from -0.375 to 0.375
- tower_weight: float32 [2, 256], replicated, may hold values from -0.375 to 0.375
- tower_bias: float32 [2], replicated, may hold values from -3 to 3
- bag_rows: int32 [16384], P(('expert', 'dp')), may hold values from 0 to 1023
- bag_sample: int32 [16384], P(('expert', 'dp')), may hold values from 0 to 255
- bag_weight: float32 [16384], P(('expert', 'dp')), may hold values from 0.5 to 2
- row_table: float32 [16384, 256], P('expert'), may hold values from -6 to 6
Outputs:
- in_grad: float32 [16, 4096, 256], P('expert', 'dp')
- out_grad: float32 [16, 4096, 256], P('expert', 'dp')
- gate_grad: float32 [16, 2, 256], P('expert')
- tower_grad: float32 [2, 256], replicated
- new_table: float32 [16384, 256], P('expert')
The draws below stay inside these ranges and needn't reach their ends.
Inputs may be any that keep to these rules, and one draw needn't show every extreme that they name: `routes`: within each device's 256 rows no expert is named more than 48 times, a bound that some block reaches; a row's two experts differ.
All inputs are finite; a program needn't handle non-finite values.
Results may differ from the reference program's by a relative error of at most 0.0041.
Values may be sent and summed in bfloat16 or wider, within the bound.
A program may use at most 128 MiB of HBM per device.

```python
import math
import jax
import jax.numpy as jnp
import numpy as np
from jax import lax

FEAT = 256
HIDDEN_SIZE = 4096
TASKS = 2
TOK_DEV = 256
BAG_DEV = 512
TROWS_DEV = 1024
EXPERTS = 16
CAP = 48
PER_OWNER = 32
TOKENS = 8192
BAG_ALL = 16384
TROWS_ALL = 16384
N_EXPERT = 16
N_DP = 2


def place_ends(values, stream_key, low, top_value):
    index_at = [jax.random.randint(jax.random.fold_in(stream_key, axis), (), 0, length) for axis, length in enumerate(values.shape)]
    widest = values.shape.index(max(values.shape))
    beside = index_at[:widest] + [(index_at[widest] + 1) % values.shape[widest]] + index_at[widest + 1:]
    return values.at[tuple(index_at)].set(low).at[tuple(beside)].set(top_value)


def block_levels(stream_key, dims, split, low, high):
    gain, own = 1.0, jax.random.fold_in(stream_key, 6)
    for position, shards_of in split:
        steps = jnp.exp(jax.random.uniform(jax.random.fold_in(own, position), (shards_of,), jnp.float32, low / len(split), high / len(split)))
        gain = gain * jnp.repeat(steps, dims[position] // shards_of).reshape([-1 if axis == position else 1 for axis in range(len(dims))])
    return gain


def assign_block(rng, own, number, rows, number_of, top, limit, skew):
    order = jax.random.permutation(rng, number_of)
    crowded, ordinary = load_shares(number_of, rows * top, limit, skew, True), load_shares(number_of, rows * top, limit, skew, False)
    places = jnp.arange(number_of)

    def named(tallies, rotation):
        used = int((tallies > 0).sum())
        fixed = max(1, used // 4)
        shifted = fixed + (places - fixed + rotation * (used - fixed)) % max(1, number_of - fixed)
        return jnp.zeros((number_of,), jnp.int32).at[order[jnp.where(places < fixed, places, shifted)]].set(jnp.asarray(tallies, jnp.int32))

    tallies = jnp.where(number % 4 == 0, named(crowded, number // 4), named(ordinary, number - number // 4 - 1))
    mixed = jax.random.permutation(jax.random.fold_in(own, 3), number_of)
    giver, sink = mixed[0:number_of // 2 * 2:2], mixed[1:number_of // 2 * 2:2]
    room = jnp.minimum(tallies[giver] - 1, limit - tallies[sink]) // 2
    room = jnp.where((giver == order[0]) | (sink == order[0]) | (tallies[sink] == 0), 0, jnp.maximum(room, 0))
    shifted = jax.random.randint(jax.random.fold_in(own, 4), (number_of // 2,), 0, 1 << 20) % (room + 1)
    tallies = tallies.at[giver].add(-shifted).at[sink].add(shifted)
    items = jnp.searchsorted(jnp.cumsum(tallies), jnp.arange(rows * top), side="right").astype(jnp.int32)
    listing = items.reshape(top, rows).T
    listing = listing[jax.random.permutation(jax.random.fold_in(own, 1), rows)]
    rotation = jax.random.randint(jax.random.fold_in(own, 2), (rows, 1), 0, top)
    return jnp.take_along_axis(listing, (jnp.arange(top)[None, :] + rotation) % top, axis=1)


def load_shares(count, total, bound, lean, full):
    portions = [(1 << 20) // math.isqrt(grade ** lean) + 1 for grade in range(1, count + 1)]
    largest = bound if full else min(bound, max(-(-total // count), total * portions[0] // sum(portions)))
    least = 1 if total - largest >= count - 1 else 0
    given, spare = [largest] + [least] * (count - 1), total - largest - least * (count - 1)
    while spare > 0:
        candidates = [i for i in range(1, count) if given[i] < largest] or [i for i in range(1, count) if given[i] < bound]
        pool, budget = sum([portions[i] for i in candidates]), spare
        for i in candidates:
            more = min(bound - given[i], max(1, budget * portions[i] // pool), spare)
            given[i] = given[i] + more
            spare = spare - more
    return np.array(given)


def noise(own_key, shape, deviation, most, pieces=(), held_as=jnp.bfloat16):
    array = jax.random.normal(own_key, shape, jnp.float32) * deviation
    if len(pieces) > 0:
        array = block_levels(own_key, shape, pieces, -0.22, 0.18) * array
    return jnp.clip(array, min=-most, max=most).astype(held_as)


def setup_inputs(seed: int = 0) -> dict:
    arg_keys = jax.random.split(jax.random.key(seed), 13)
    pooled = noise(arg_keys[0], (TOKENS, FEAT), 1.0, 6.0, ((0, 32),))
    routes_keys = jax.random.split(jax.random.fold_in(arg_keys[1], 1), TOKENS // TOK_DEV)
    routes_turns = jax.random.permutation(jax.random.fold_in(arg_keys[1], 3), TOKENS // TOK_DEV)
    routes = jax.vmap(lambda own, number: assign_block(jax.random.fold_in(arg_keys[1], 2), own, number, TOK_DEV, EXPERTS, 2, CAP, 2))(routes_keys, routes_turns).reshape((TOKENS, 2))
    labels = place_ends(jax.random.randint(arg_keys[2], (TOKENS, TASKS), 0, 2), jax.random.fold_in(arg_keys[2], 1), 0, 1).astype(jnp.int32)
    in_weight = noise(arg_keys[3], (EXPERTS, HIDDEN_SIZE, FEAT), FEAT ** -0.5, 0.375, ((0, 16),))
    out_weight = noise(arg_keys[4], (EXPERTS, HIDDEN_SIZE, FEAT), HIDDEN_SIZE ** -0.5, 0.09375, ((0, 16),))
    gate_weight = noise(arg_keys[5], (EXPERTS, TASKS, FEAT), FEAT ** -0.5, 0.375)
    tower_weight = noise(arg_keys[6], (TASKS, FEAT), FEAT ** -0.5, 0.375, (), jnp.float32)
    tower_bias = noise(arg_keys[7], (TASKS,), 1.0, 3.0, (), jnp.float32)
    bag_rows = place_ends(jax.random.randint(arg_keys[8], (BAG_ALL,), 0, TROWS_DEV), jax.random.fold_in(arg_keys[8], 1), 0, TROWS_DEV - 1).astype(jnp.int32)
    bag_sample = place_ends(jax.random.randint(arg_keys[9], (BAG_ALL,), 0, TOK_DEV), jax.random.fold_in(arg_keys[9], 1), 0, TOK_DEV - 1).astype(jnp.int32)
    bag_weight = jnp.clip(jnp.exp(math.log(2.0) - 1.3862944 * jax.random.uniform(arg_keys[10], (BAG_ALL,), jnp.float32) ** block_levels(arg_keys[10], (BAG_ALL,), ((0, 32),), -0.2, 0.2)), 0.5, 2.0)
    row_table = noise(arg_keys[11], (TROWS_ALL, FEAT), 1.0, 6.0, ((0, 16),), jnp.float32)
    return {"pooled": pooled, "routes": routes, "labels": labels, "in_weight": in_weight, "out_weight": out_weight, "gate_weight": gate_weight, "tower_weight": tower_weight, "tower_bias": tower_bias, "bag_rows": bag_rows, "bag_sample": bag_sample, "bag_weight": bag_weight, "row_table": row_table}


LOSS_SCALE = 32.0
STEP_SIZE = 0.25
HIGH = lax.Precision.HIGHEST

def silu_grad(pre_silu):
    sigma = jax.nn.sigmoid(pre_silu)
    return sigma * (1.0 + pre_silu * (1.0 - sigma))

def reference(pooled, routes, labels, in_weight, out_weight, gate_weight, tower_weight, tower_bias, bag_rows, bag_sample, bag_weight, row_table):
    device_count = N_EXPERT * N_DP
    flat_routes = routes.reshape(device_count, TOK_DEV * 2)
    one_hot_int = (flat_routes[:, :, None] == jnp.arange(EXPERTS, dtype=jnp.int32)[None, None, :]).astype(jnp.int32)
    ranks = jnp.cumsum(one_hot_int, axis=1) - 1
    slot_of = lax.optimization_barrier(jnp.sum(ranks * one_hot_int, axis=2)).astype(jnp.int32)
    slot_index = (flat_routes * CAP + slot_of).astype(jnp.int32)

    def scatter_rows(values):
        empty = jnp.zeros((device_count, EXPERTS * CAP, FEAT), jnp.bfloat16)
        filled = jax.vmap(lambda buffer, where, rows_in: buffer.at[where].set(rows_in))(empty, slot_index, values)
        return filled.reshape(device_count, EXPERTS, CAP, FEAT).transpose(1, 0, 2, 3).reshape(EXPERTS, device_count * CAP, FEAT)

    def collect_rows(values):
        back = values.reshape(EXPERTS, device_count, CAP, FEAT).transpose(1, 0, 2, 3).reshape(device_count, EXPERTS * CAP, FEAT)
        picked = jax.vmap(lambda buffer, where: buffer[where])(back, slot_index)
        return picked.reshape(TOKENS, 2, FEAT)
    paired = jnp.repeat(pooled.reshape(device_count, TOK_DEV, FEAT), 2, axis=1)
    routed_in = scatter_rows(paired)

    def forward(items):
        inputs, in_matrix, out_matrix = items
        pre_silu = lax.dot_general(inputs, in_matrix, (((1,), (1,)), ((), ())), preferred_element_type=jnp.float32)
        hidden_act = jax.nn.silu(pre_silu).astype(jnp.bfloat16)
        return jnp.dot(hidden_act, out_matrix, preferred_element_type=jnp.float32).astype(jnp.bfloat16)
    expert_rows = lax.map(forward, (routed_in, in_weight, out_weight))
    expert_out = collect_rows(expert_rows).astype(jnp.float32)
    one_hot = (routes[:, :, None] == jnp.arange(EXPERTS, dtype=jnp.int32)[None, None, :]).astype(jnp.float32)
    gate_flat = gate_weight.reshape(EXPERTS * TASKS, FEAT)
    all_logits = lax.dot_general(pooled, gate_flat, (((1,), (1,)), ((), ())), preferred_element_type=jnp.float32).reshape(TOKENS, EXPERTS, TASKS)
    chosen = jnp.einsum('nke,net->ntk', one_hot, all_logits, precision=HIGH)
    gate_first = jax.nn.sigmoid(chosen[:, :, 0] - chosen[:, :, 1])
    gate_second = 1.0 - gate_first
    mixture = gate_first[:, :, None] * expert_out[:, None, 0, :] + gate_second[:, :, None] * expert_out[:, None, 1, :]
    task_logit = lax.optimization_barrier(jnp.sum(mixture * tower_weight[None], axis=2)) + tower_bias[None]
    logit_grad = LOSS_SCALE * (jax.nn.sigmoid(task_logit) - labels.astype(jnp.float32))
    tower_grad = jnp.einsum('nt,ntf->tf', logit_grad, mixture, precision=HIGH)
    mixture_grad = logit_grad[:, :, None] * tower_weight[None]
    routed_grad = jnp.stack([lax.optimization_barrier(jnp.sum(gate_first[:, :, None] * mixture_grad, axis=1)), lax.optimization_barrier(jnp.sum(gate_second[:, :, None] * mixture_grad, axis=1))], axis=1).astype(jnp.bfloat16)
    gate_dot = jnp.einsum('ntf,nkf->ntk', mixture_grad, expert_out, precision=HIGH)
    first_grad = (gate_dot[:, :, 0] - gate_dot[:, :, 1]) * gate_first * gate_second
    select_grad = jnp.stack([first_grad, -first_grad], axis=2)
    mix_table = jnp.einsum('nke,ntk->net', one_hot, select_grad, precision=HIGH).reshape(TOKENS, EXPERTS * TASKS)
    gate_grad = lax.dot_general(mix_table, pooled.astype(jnp.float32), (((0,), (0,)), ((), ())), precision=HIGH).reshape(EXPERTS, TASKS, FEAT)
    gate_input = jnp.dot(mix_table, gate_flat.astype(jnp.float32), precision=HIGH)
    routed_back = scatter_rows(routed_grad.reshape(device_count, TOK_DEV * 2, FEAT))

    def backward(items):
        inputs, grad_rows, in_matrix, out_matrix = items
        pre_silu = lax.dot_general(inputs, in_matrix, (((1,), (1,)), ((), ())), preferred_element_type=jnp.float32)
        hidden_act = jax.nn.silu(pre_silu).astype(jnp.bfloat16)
        hidden_grad = lax.dot_general(grad_rows, out_matrix, (((1,), (1,)), ((), ())), preferred_element_type=jnp.float32)
        pre_grad = (hidden_grad * silu_grad(pre_silu)).astype(jnp.bfloat16)
        in_part = lax.dot_general(pre_grad, inputs, (((0,), (0,)), ((), ())), preferred_element_type=jnp.float32)
        out_part = lax.dot_general(hidden_act, grad_rows, (((0,), (0,)), ((), ())), preferred_element_type=jnp.float32)
        input_grad = jnp.dot(pre_grad, in_matrix, preferred_element_type=jnp.float32).astype(jnp.bfloat16)
        return (in_part, out_part, input_grad)
    in_grad, out_grad, input_rows = lax.map(backward, (routed_in, routed_back, in_weight, out_weight))
    input_grad = collect_rows(input_rows).astype(jnp.float32)
    pooled_grad = gate_input + input_grad[:, 0] + input_grad[:, 1]
    entry = jnp.arange(BAG_ALL, dtype=jnp.int32)
    block_of = entry // BAG_DEV
    owner_of = entry % BAG_DEV // PER_OWNER
    sample_of = (block_of * TOK_DEV + bag_sample).astype(jnp.int32)
    row_grad = (bag_weight[:, None] * pooled_grad[sample_of]).astype(jnp.bfloat16)
    target = (owner_of * TROWS_DEV + bag_rows).astype(jnp.int32)
    row_sums = jax.ops.segment_sum(row_grad.astype(jnp.float32), target, num_segments=TROWS_ALL)
    new_table = row_table - STEP_SIZE * row_sums
    return (in_grad, out_grad, gate_grad, tower_grad, new_table)
```

```python
import functools

import jax
import jax.numpy as jnp
from jax import lax
from jax.experimental import pallas as pl
from jax.experimental.pallas import tpu as pltpu
from jax.sharding import PartitionSpec as P

LOSS_SCALE = 32.0
STEP_SIZE = 0.25
F32, BF16 = jnp.float32, jnp.bfloat16
MESH = pl.DeviceIdType.MESH
VMEM_LIMIT = 56 * 2**20
SLOT_BASE = 4096


def mm(left, right, left_dim=1, right_dim=0):
    return lax.dot_general(
        left, right, (((left_dim,), (right_dim,)), ((), ())), preferred_element_type=F32
    )


def nt(left, right):
    return mm(left, right, 1, 1)


def halves(value):
    high = value.astype(BF16).astype(F32)
    return high, value - high


def stacked(value):
    return jnp.concatenate(halves(value), axis=0).astype(BF16)


def folded(value):
    half = value.shape[0] // 2
    return value[:half] + value[half:]


def sigmoid(value):
    return 0.5 * jnp.tanh(0.5 * value) + 0.5


def iota(shape, dim):
    return lax.broadcasted_iota(jnp.int32, shape, dim)


def one_hot(condition):
    return jnp.where(condition, 1.0, 0.0)


def lane_pack(pieces, width, lanes):
    lane = iota(pieces[0].shape, 1)
    rolled = [pltpu.roll(p, i * width % 128, 1) if i * width % 128 else p for i, p in enumerate(pieces)]
    parts = []
    for start in range(0, lanes, 128):
        total = jnp.zeros_like(pieces[0])
        for i, piece in enumerate(rolled):
            low, high = i * width - start, (i + 1) * width - start
            if high > 0 and low < 128:
                total = jnp.where((lane >= low) & (lane < high), piece, total)
        parts.append(total)
    return jnp.concatenate(parts, axis=1)


def kernel(
    sizes,
    pooled_hbm,
    routes_hbm,
    labels_hbm,
    in_hbm,
    out_hbm,
    gate_hbm,
    tower_hbm,
    bias_hbm,
    bag_rows_hbm,
    bag_sample_hbm,
    bag_weight_hbm,
    table_hbm,
    in_sum_ref,
    out_sum_ref,
    gate_sum_ref,
    tower_sum_ref,
    table_ref,
    pooled_ref,
    routes_rows_ref,
    labels_ref,
    gate_ref,
    tower_ref,
    bias_ref,
    bag_rows_ref,
    bag_sample_ref,
    bag_weight_ref,
    in_ref,
    out_ref,
    turned_ref,
    proj_rows_ref,
    proj_cols_ref,
    act_ref,
    slope_ref,
    pre_ref,
    bag_place_ref,
    bag_acc,
    bag_weights,
    a_send,
    a_recv,
    m_send,
    m_recv,
    b_send,
    b_recv,
    d_send,
    d_recv,
    e_send,
    e_recv,
    e_other,
    t_send,
    t_recv,
    s_send,
    s_recv,
    rows_mine,
    rows_other,
    hidden_mine,
    hidden_other,
    hidden_recv,
    rows_acc,
    back_acc,
    send_sem,
    recv_sem,
    dp_send,
    dp_recv,
    local_sem,
):
    count, cap, chunk, chunks, per_owner = sizes
    rows_all = count * cap
    tok_rows, feature = pooled_hbm.shape
    me, core = lax.axis_index("expert"), lax.axis_index("dp")
    other = 1 - core
    half = chunks // 2
    group = count // 2
    slots = group * cap
    blocks = slots // 128
    near = lax.div(me, group)
    far = 1 - near
    place_in = lax.rem(me, group)
    held = e_send.shape[1]
    entries = count * held

    def remote(phase, peer, source, target):
        return pltpu.make_async_remote_copy(
            src_ref=source,
            dst_ref=target,
            send_sem=send_sem.at[phase, peer],
            recv_sem=recv_sem.at[phase, me],
            device_id={"expert": peer},
            device_id_type=MESH,
        )

    def arrival(phase, peer, source, target):
        return pltpu.make_async_remote_copy(
            src_ref=source,
            dst_ref=target,
            send_sem=send_sem.at[phase, peer],
            recv_sem=recv_sem.at[phase, peer],
            device_id={"expert": peer},
            device_id_type=MESH,
        )

    def peers(which, act):
        if which == "far":

            @pl.loop(0, group)
            def _(step):
                act(far * group + lax.rem(place_in + step, group))

        else:

            @pl.loop(1, group)
            def _(step):
                act(near * group + lax.rem(place_in + step, group))

    def everyone(act):
        peers("far", act)
        peers("near", act)

    def to_other(index, source, target):
        return pltpu.make_async_remote_copy(
            src_ref=source,
            dst_ref=target,
            send_sem=dp_send.at[index],
            recv_sem=dp_recv.at[index],
            device_id={"dp": other},
            device_id_type=MESH,
        )

    def a_copy(make, peer):
        return make(0, peer, a_send.at[peer], a_recv.at[me if make is remote else peer])

    def m_copy(make, peer):
        return make(1, peer, m_send.at[peer], m_recv.at[me if make is remote else peer])

    def b_copy(make, peer, index):
        return make(2 + index, peer, b_send.at[index], b_recv.at[me if make is remote else peer, index])

    def d_copy(make, peer):
        return make(4, peer, d_send.at[peer], d_recv.at[me if make is remote else peer])

    def e_copy(make, peer):
        return make(5, peer, e_send.at[peer], e_recv.at[me if make is remote else peer])

    def t_copy(make, peer):
        return make(6, peer, t_send, t_recv.at[me if make is remote else peer])

    barrier = pltpu.get_barrier_semaphore()

    @pl.loop(1, count)
    def _(step):
        pl.semaphore_signal(
            barrier, inc=1, device_id={"expert": lax.rem(me + step, count)}, device_id_type=MESH
        )

    pl.semaphore_signal(barrier, inc=1, device_id={"dp": other}, device_id_type=MESH)
    loads = [
        pltpu.make_async_copy(source, target, local_sem.at[index])
        for index, (source, target) in enumerate(
            (
                (routes_hbm, routes_rows_ref),
                (pooled_hbm, pooled_ref),
                (labels_hbm, labels_ref),
                (bag_rows_hbm, bag_rows_ref),
                (tower_hbm, tower_ref),
                (out_hbm, out_ref),
                (in_hbm, in_ref),
                (gate_hbm, gate_ref),
                (bias_hbm, bias_ref),
                (bag_sample_hbm, bag_sample_ref),
                (bag_weight_hbm, bag_weight_ref),
                (table_hbm, table_ref),
            )
        )
    ]
    for load in loads:
        load.start()
    loads[0].wait()

    first_row, second_row = routes_rows_ref[0:1, :], routes_rows_ref[1:2, :]
    first_map = one_hot(iota((count, tok_rows), 0) == first_row)
    second_map = one_hot(iota((count, tok_rows), 0) == second_row)
    above = one_hot(
        iota((tok_rows, tok_rows), 0) < iota((tok_rows, tok_rows), 1)
    ).astype(BF16)
    before = mm(jnp.concatenate([first_map, second_map], axis=0).astype(BF16), above)
    first_total = jnp.sum(first_map, axis=1, keepdims=True)
    first_rank = jnp.sum(first_map * before[:count], axis=0, keepdims=True).astype(jnp.int32)
    second_rank = jnp.sum(
        second_map * (before[count:] + first_total), axis=0, keepdims=True
    ).astype(jnp.int32)
    first_slot = first_rank + first_row * cap
    second_slot = second_rank + second_row * cap

    def fill_of(index):
        places = iota((slots, tok_rows), 0) + index * slots
        return one_hot((places == first_slot) | (places == second_slot)).astype(BF16)

    def send_half(index):
        rows = 0.5 * mm(fill_of(index), pooled_ref[...])
        a_send[pl.ds(index * group, group)] = rows.astype(BF16).reshape(group, cap, feature)

    loads[1].wait()
    send_half(near)
    pl.semaphore_wait(barrier, count)
    peers("near", lambda peer: a_copy(remote, peer).start())
    send_half(far)
    peers("far", lambda peer: a_copy(remote, peer).start())
    a_recv[me] = a_send[me]
    for load in loads[2:5]:
        load.wait()

    lanes = iota((128, tok_rows), 0)
    first_at = one_hot(lanes == first_rank).astype(BF16)
    second_at = one_hot(lanes == second_rank).astype(BF16)
    label_code = 2 * labels_ref[0:1, :] + labels_ref[1:2, :] + 1

    def partner(own_map, row, rank):
        code = (4 * rank + label_code).astype(F32)
        return jnp.concatenate([own_map * row.astype(F32), own_map * code], axis=0).astype(BF16)

    told = nt(partner(first_map, second_row, second_rank), first_at) + nt(
        partner(second_map, first_row, first_rank), second_at
    )
    code = told[count:]
    meta = jnp.where(
        code > 0.0, SLOT_BASE * told[:count] + code + (4 * cap * place_in).astype(F32), 0.0
    )
    piece_lane = iota((1, 128), 1)
    for owner in range(count):
        start = owner * per_owner
        line = bag_rows_ref[start // 128 : start // 128 + 1, :].astype(F32)
        if start % 128:
            line = pltpu.roll(jnp.broadcast_to(line, (8, 128)), 128 - start % 128, 1)[0:1, :]
        m_send[owner, 0:1, :] = meta[owner : owner + 1, :]
        m_send[owner, 1:2, :] = jnp.where(piece_lane < per_owner, line, -1.0)
    everyone(lambda peer: m_copy(remote, peer).start())
    m_recv[me] = m_send[me]

    feat_row = iota((8, feature), 0)
    tower_rows = jnp.where(
        feat_row == 0, tower_ref[0:1, :], jnp.where(feat_row == 1, tower_ref[1:2, :], 0.0)
    )
    tower_high, tower_low = halves(tower_rows)
    tower_high, tower_low = tower_high.astype(BF16), tower_low.astype(BF16)
    for load in loads[5:11]:
        load.wait()

    @pl.loop(0, chunks)
    def _(step):
        span = pl.ds(pl.multiple_of(step * chunk, chunk), chunk)
        weights = out_ref[span, :]
        proj_rows_ref[step] = stacked(nt(tower_high, weights) + nt(tower_low, weights))
        cols = nt(weights, tower_high) + nt(weights, tower_low)
        proj_cols_ref[0, span, :] = jnp.broadcast_to(cols[:, 0:1], (chunk, 128))
        proj_cols_ref[1, span, :] = jnp.broadcast_to(cols[:, 1:2], (chunk, 128))
        turned_ref[step] = in_ref[span, :].T

    rows_acc[...] = jnp.zeros_like(rows_acc)
    back_acc[...] = jnp.zeros_like(back_acc)

    def forward(index):
        lane_span = pl.ds(pl.multiple_of(index * slots, 128), slots)
        features = a_recv.at[pl.ds(index * group, group)]

        @pl.loop(0, chunks)
        def _(step):
            span = pl.ds(pl.multiple_of(step * chunk, chunk), chunk)
            close = nt(in_ref[span, :], features[...].reshape(slots, feature))
            bend = jnp.tanh(close)
            bent = close * bend
            slope_ref[span, lane_span] = (1.0 + bend) + (close - bent * bend)
            act = (close + bent).astype(BF16)
            act_ref[span, lane_span] = act
            rows_acc[:, lane_span] += mm(proj_rows_ref[step], act)

        dots = folded(rows_acc[:, lane_span])
        tile_row = iota((8, 128), 0)
        tile = jnp.zeros((8, 128), F32)
        for task in range(2):
            for block in range(blocks):
                piece = dots[task : task + 1, block * 128 : (block + 1) * 128]
                tile = jnp.where(tile_row == task * blocks + block, piece, tile)
        b_send[index] = tile
        b_recv[me, index] = tile
        everyone(lambda peer: b_copy(remote, peer, index).start())

    peers("near", lambda peer: a_copy(arrival, peer).wait_recv())
    forward(near)
    peers("far", lambda peer: a_copy(arrival, peer).wait_recv())
    forward(far)

    everyone(lambda peer: m_copy(arrival, peer).wait_recv())
    pieces = [m_recv[source] for source in range(count)]
    told = jnp.concatenate(
        [lane_pack(pieces[i * group : (i + 1) * group], cap, slots)[0:1, :] for i in range(2)],
        axis=1,
    ).astype(jnp.int32)
    bag_lanes = -(-entries // 128) * 128
    rows_mine[...] = jnp.broadcast_to(
        lane_pack(pieces, held, bag_lanes)[1:2, :entries], rows_mine.shape
    )
    rows_copy = to_other(2, rows_mine, rows_other)
    rows_copy.start()
    valid = told > 0
    pair_expert = lax.shift_right_logical(told, 12)
    pair_code = jnp.bitwise_and(told, SLOT_BASE - 1) - 1
    pair_slot = lax.shift_right_logical(pair_code, 2)
    row_wide = iota((8, rows_all), 0)
    slot_labels = jnp.where(
        row_wide == 0,
        jnp.bitwise_and(lax.shift_right_logical(pair_code, 1), 1),
        jnp.bitwise_and(pair_code, 1),
    ).astype(F32)

    def dot_key(expert, slot):
        lane_of = one_hot(
            iota((128, slot.shape[1]), 0) == jnp.bitwise_and(slot, 127)
        ).astype(BF16)
        return lane_of, expert * 8 + lax.shift_right_logical(slot, 7)

    def look_up(tiles, key):
        lane_of, row_of_key = key
        found = folded(mm(tiles, lane_of))
        rows = iota(found.shape, 0)
        return [
            jnp.sum(
                jnp.where(rows == row_of_key + task * blocks, found, 0.0), axis=0, keepdims=True
            )
            for task in range(2)
        ]

    pair_key = dot_key(pair_expert, pair_slot)
    gates = [gate_ref[:, task, :] for task in range(2)]
    expert_row = iota((count, rows_all), 0)
    sign = one_hot(expert_row == me) - one_hot(expert_row == pair_expert)
    features_all = a_recv[...].reshape(rows_all, feature)
    slot_gate = jnp.zeros((8, rows_all), F32)
    for task in range(2):
        logits = nt(gates[task], features_all)
        slot_gate = jnp.where(
            row_wide == task, jnp.sum(sign * logits, axis=0, keepdims=True), slot_gate
        )
    own_gate = 0.5 * jnp.tanh(slot_gate) + 0.5
    pair_gate = 1.0 - own_gate
    gate_both = own_gate * pair_gate
    slot_bias = jnp.where(row_wide == 0, bias_ref[0], bias_ref[1])

    row_of = iota((8, tok_rows), 0)
    labels = jnp.where(row_of == 0, labels_ref[0:1, :], labels_ref[1:2, :]).astype(F32)
    bias = jnp.where(row_of == 0, bias_ref[0], bias_ref[1])
    signed = first_map - second_map
    gate_logit = jnp.zeros((8, tok_rows), F32)
    for task in range(2):
        logits = nt(gates[task], pooled_ref[...])
        gate_logit = jnp.where(
            row_of == task, jnp.sum(signed * logits, axis=0, keepdims=True), gate_logit
        )
    gate_first = sigmoid(gate_logit)
    gate_second = 1.0 - gate_first
    first_key = dot_key(first_row, first_rank + cap * place_in)
    second_key = dot_key(second_row, second_rank + cap * place_in)
    sample_wide = jnp.broadcast_to(bag_sample_ref[...].astype(F32), (8, entries))
    weight_wide = jnp.broadcast_to(bag_weight_ref[...], (8, entries))
    sample_col, weight_col = sample_wide.T[:, 0:1], weight_wide.T[:, 0:1]
    bag = one_hot(iota((entries, tok_rows), 1) == sample_col.astype(jnp.int32)).astype(BF16)
    for index in range(2):
        bag_place_ref[:, index * slots : (index + 1) * slots] = nt(bag, fill_of(index)).astype(BF16)

    for index in range(2):
        everyone(lambda peer, index=index: b_copy(arrival, peer, index).wait_recv())

    own_dot = folded(rows_acc[...])
    pair_dot = []
    for index in range(2):
        lane_span = slice(index * slots, (index + 1) * slots)
        tiles = stacked(b_recv[:, index].reshape(count * 8, 128))
        found = look_up(tiles, (pair_key[0][:, lane_span], pair_key[1][:, lane_span]))
        pair_dot.append(jnp.where(iota((8, slots), 0) == 0, found[0], found[1]))
    pair_dot = jnp.concatenate(pair_dot, axis=1)
    task_logit = own_gate * own_dot + pair_gate * pair_dot + slot_bias
    logit_grad = jnp.where(valid, LOSS_SCALE * (sigmoid(task_logit) - slot_labels), 0.0)
    gate_grad = pltpu.roll(logit_grad * (own_dot - pair_dot) * gate_both, 2, 0)
    coefs = jnp.where(
        row_wide < 2, own_gate * logit_grad, jnp.where(row_wide < 4, gate_grad, 0.0)
    )
    rows_acc[0:8, :] = coefs

    def backward(index):
        lane_span = pl.ds(pl.multiple_of(index * slots, 128), slots)
        coef_zero, coef_one = rows_acc[0:1, lane_span], rows_acc[1:2, lane_span]

        @pl.loop(0, chunks)
        def _(step):
            span = pl.ds(pl.multiple_of(step * chunk, chunk), chunk)
            zero, one = (
                jnp.concatenate([proj_cols_ref[task, span, :]] * blocks, axis=1) for task in range(2)
            )
            hidden_grad = zero * coef_zero + one * coef_one
            grad = (hidden_grad * slope_ref[span, lane_span]).astype(BF16)
            pre_ref[span, lane_span] = grad
            back_acc[:, lane_span] += mm(turned_ref[step], grad)

        back = 0.5 * back_acc[:, lane_span].T
        d_send[pl.ds(index * group, group)] = back.astype(BF16).reshape(group, cap, feature)

    backward(far)
    peers("far", lambda peer: d_copy(remote, peer).start())
    backward(near)
    peers("near", lambda peer: d_copy(remote, peer).start())
    d_recv[me] = d_send[me]

    coef_rows = stacked(coefs)
    half_rows = half * chunk
    in_other = slope_ref.at[pl.ds(0, half_rows), pl.ds(0, feature)]
    in_mine = slope_ref.at[pl.ds(half_rows, half_rows), pl.ds(0, feature)]

    def weight_chunk(step, in_target, hidden_target, slot):
        span = pl.ds(pl.multiple_of(step * chunk, chunk), chunk)
        in_target[pl.ds(pl.multiple_of(slot * chunk, chunk), chunk), :] = mm(
            pre_ref[span, :], a_recv[...].reshape(rows_all, feature)
        )
        hidden = folded(nt(coef_rows, act_ref[span, :]))
        hidden_target[slot] = hidden
        return folded(mm(stacked(hidden), out_ref[span, :]))

    tower = jnp.zeros((8, feature), F32)
    tower = lax.fori_loop(
        0,
        half,
        lambda i, total: total + weight_chunk(other * half + i, in_other, hidden_other, i),
        tower,
    )
    in_copy = to_other(0, in_other, in_sum_ref)
    hidden_copy = to_other(1, hidden_other, hidden_recv)
    in_copy.start()
    hidden_copy.start()
    tower = lax.fori_loop(
        0,
        half,
        lambda i, total: total + weight_chunk(core * half + i, in_mine, hidden_mine, i),
        tower,
    )
    t_send[...] = tower[0:2]
    t_recv[me] = tower[0:2]
    everyone(lambda peer: t_copy(remote, peer).start())
    gate = 2.0 * folded(mm(coef_rows, a_recv[...].reshape(rows_all, feature)))

    tiles = stacked(b_recv[:, near].reshape(count * 8, 128))

    def at_home(key):
        found = look_up(tiles, key)
        return jnp.where(row_of == 0, found[0], found[1])

    first_dot, second_dot = at_home(first_key), at_home(second_key)
    task_logit = gate_first * first_dot + gate_second * second_dot + bias
    logit_grad = LOSS_SCALE * (sigmoid(task_logit) - labels)
    first_grad = logit_grad * (first_dot - second_dot) * gate_first * gate_second
    gate_input = jnp.zeros((tok_rows, feature), F32)
    for task in range(2):
        high, low = halves(signed * first_grad[task : task + 1, :])
        gate_input += mm(high.astype(BF16), gates[task], 0, 0)
        gate_input += mm(low.astype(BF16), gates[task], 0, 0)
    high, low = halves(gate_input)
    bag_acc[...] = mm(bag, high.astype(BF16)) + mm(bag, low.astype(BF16))

    everyone(lambda peer: a_copy(remote, peer).wait_send())
    everyone(lambda peer: m_copy(remote, peer).wait_send())
    for index in range(2):
        everyone(lambda peer, index=index: b_copy(remote, peer, index).wait_send())

    def bag_part(row_span, index):
        lane_span = pl.ds(pl.multiple_of(index * slots, 128), slots)
        back = d_recv[pl.ds(index * group, group)].reshape(slots, feature)
        return mm(bag_place_ref[row_span, lane_span], back)

    peers("near", lambda peer: d_copy(arrival, peer).wait_recv())
    bag_acc[...] += bag_part(pl.ds(0, entries), near)
    weight_lanes = jnp.broadcast_to(weight_col, (entries, 128))
    match_rows = entries // 2
    bag_weights[...] = weight_lanes
    peers("far", lambda peer: d_copy(arrival, peer).wait_recv())
    for which, index in (("far", far), ("near", near)):
        row_span = pl.ds(pl.multiple_of(index * match_rows, 8), match_rows)
        weights = jnp.concatenate([bag_weights[row_span, :]] * (feature // 128), axis=1)
        rows = weights * (bag_acc[row_span, :] + bag_part(row_span, far))
        e_send[pl.ds(index * group, group)] = rows.astype(BF16).reshape(group, held, feature)
        peers(which, lambda peer: e_copy(remote, peer).start())

    def forwarded(peer, source):
        return to_other(4 + peer, source, e_other.at[peer])

    e_recv[me] = e_send[me]
    forwarded(me, e_send.at[me]).start()

    hidden_copy.wait()
    tower_three = jnp.concatenate(
        [tower_high.astype(F32), tower_low.astype(F32), tower_high.astype(F32)], axis=0
    ).astype(BF16)

    @pl.loop(0, half)
    def _(step):
        span = pl.ds(pl.multiple_of(step * chunk, chunk), chunk)
        high, low = halves(hidden_mine[step] + hidden_recv[step])
        three = jnp.concatenate([high, high, low], axis=0).astype(BF16)
        out_sum_ref[span, :] = mm(three, tower_three, 0, 0)

    everyone(lambda peer: t_copy(arrival, peer).wait_recv())
    summed = t_recv[0]
    for source in range(1, count):
        summed = summed + t_recv[source]
    mine = jnp.concatenate([summed, gate[2:4], jnp.zeros((4, feature), F32)], axis=0)
    s_send[...] = mine
    small_copy = to_other(3, s_send, s_recv)
    small_copy.start()
    in_copy.wait()

    @pl.loop(0, half)
    def _(step):
        span = pl.ds(pl.multiple_of(step * chunk, chunk), chunk)
        in_sum_ref[span, :] = in_sum_ref[span, :] + in_mine[span, :]

    everyone(lambda peer: d_copy(remote, peer).wait_send())
    everyone(lambda peer: t_copy(remote, peer).wait_send())
    rows_copy.wait()
    loads[11].wait()
    table_rows = table_ref.shape[0]
    part = table_rows // 4
    sides = ((rows_mine, e_recv, pre_ref.at[pl.ds(0, table_rows), pl.ds(0, entries)]),)
    sides += ((rows_other, e_other, pre_ref.at[pl.ds(table_rows, table_rows), pl.ds(0, entries)]),)

    @pl.loop(0, 4)
    def _(step):
        span = pl.ds(pl.multiple_of(step * part, part), part)
        rows = (iota((part, entries), 0) + step * part).astype(F32)
        for rows_ref, _, match_ref in sides:
            match_ref[span, :] = one_hot(rows == rows_ref[0:1, :]).astype(BF16)

    def gather(side, index):
        _, source_ref, match_ref = side
        sources = source_ref[pl.ds(index * group, group)].reshape(group * held, feature)
        lane_span = pl.ds(pl.multiple_of(index * (entries // 2), 128), entries // 2)

        @pl.loop(0, 4)
        def _(step):
            span = pl.ds(pl.multiple_of(step * part, part), part)
            table_ref[span, :] = table_ref[span, :] - STEP_SIZE * mm(
                match_ref[span, lane_span], sources
            )

    def landed(peer):
        e_copy(arrival, peer).wait_recv()
        forwarded(peer, e_recv.at[peer]).start()

    def crossed(peer):
        forwarded(peer, e_recv.at[peer]).wait()

    peers("near", landed)
    gather(sides[0], near)
    peers("near", crossed)
    crossed(me)
    gather(sides[1], near)
    peers("far", landed)
    gather(sides[0], far)
    small_copy.wait()
    both = mine + s_recv[...]
    tower_sum_ref[...] = both[0:2]
    gate_sum_ref[...] = both[2:4]
    everyone(lambda peer: e_copy(remote, peer).wait_send())

    peers("far", crossed)
    gather(sides[1], far)


def write_out(*refs):
    sources, targets, sem = refs[:5], refs[5:10], refs[10]
    copies = []
    for source, target in zip(sources, targets, strict=True):
        parts = 4 if source.shape[0] % 32 == 0 else 1
        rows = source.shape[0] // parts
        for part in range(parts):
            span = pl.ds(part * rows, rows)
            copies.append(
                pltpu.make_async_copy(source.at[span], target.at[span], sem.at[len(copies)])
            )
            copies[-1].start()
    for copy in copies:
        copy.wait()


def on_device(
    pooled,
    routes,
    labels,
    in_weight,
    out_weight,
    gate_weight,
    tower_weight,
    tower_bias,
    bag_rows,
    bag_sample,
    bag_weight,
    row_table,
):
    count = lax.axis_size("expert")
    tok_rows, feature = pooled.shape
    tasks = tower_weight.shape[0]
    hidden = in_weight.shape[1]
    cap = -(-(3 * tok_rows // count) // 8) * 8
    rows_all = count * cap
    chunk = 1024 if rows_all * 1024 < 2**20 else 512
    chunks = hidden // chunk
    per_owner = bag_rows.shape[0] // count
    held = -(-per_owner // 8) * 8
    entries = count * held

    def bags(values, empty):
        if held == per_owner:
            return values
        return jnp.pad(
            values.reshape(count, per_owner), ((0, 0), (0, held - per_owner)), constant_values=empty
        )

    vmem = pl.BlockSpec(memory_space=pltpu.VMEM)
    anywhere = pl.BlockSpec(memory_space=pl.ANY)
    routed = (count, cap, feature)
    owned = (count, held, feature)
    half_rows = hidden // 2
    halved = (chunks // 2, 8, chunk)
    in_hbm = [
        pltpu.with_memory_space_constraint(value, pltpu.HBM)
        for value in (
            pooled,
            routes.T,
            labels.T,
            in_weight[0],
            out_weight[0],
            gate_weight,
            tower_weight,
            tower_bias,
            bag_rows.reshape(-1, 128),
            bags(bag_sample, -1).reshape(1, -1),
            bags(bag_weight, 0.0).reshape(1, -1),
            row_table,
        )
    ]
    results = pl.pallas_call(
        functools.partial(kernel, (count, cap, chunk, chunks, per_owner)),
        out_shape=(
            pltpu.VMEM((half_rows, feature), F32),
            pltpu.VMEM((half_rows, feature), F32),
            pltpu.VMEM((tasks, feature), F32),
            pltpu.VMEM((tasks, feature), F32),
            pltpu.VMEM(row_table.shape, F32),
        ),
        in_specs=[anywhere] * 12,
        out_specs=(vmem,) * 5,
        scratch_shapes=[
            pltpu.VMEM(pooled.shape, BF16),
            pltpu.VMEM((2, tok_rows), jnp.int32),
            pltpu.VMEM((2, tok_rows), jnp.int32),
            pltpu.VMEM(gate_weight.shape, BF16),
            pltpu.VMEM(tower_weight.shape, F32),
            pltpu.SMEM(tower_bias.shape, F32),
            pltpu.VMEM((bag_rows.shape[0] // 128, 128), jnp.int32),
            pltpu.VMEM((1, entries), jnp.int32),
            pltpu.VMEM((1, entries), F32),
            pltpu.VMEM((hidden, feature), BF16),
            pltpu.VMEM((hidden, feature), BF16),
            pltpu.VMEM((chunks, feature, chunk), BF16),
            pltpu.VMEM((chunks, 16, chunk), BF16),
            pltpu.VMEM((2, hidden, 128), F32),
            pltpu.VMEM((hidden, rows_all), BF16),
            pltpu.VMEM((hidden, rows_all), F32),
            pltpu.VMEM((hidden, rows_all), BF16),
            pltpu.VMEM((entries, rows_all), BF16),
            pltpu.VMEM((entries, feature), F32),
            pltpu.VMEM((entries, 128), F32),
            pltpu.VMEM(routed, BF16),
            pltpu.VMEM(routed, BF16),
            pltpu.VMEM((count, 2, 128), F32),
            pltpu.VMEM((count, 2, 128), F32),
            pltpu.VMEM((2, 8, 128), F32),
            pltpu.VMEM((count, 2, 8, 128), F32),
            pltpu.VMEM(routed, BF16),
            pltpu.VMEM(routed, BF16),
            pltpu.VMEM(owned, BF16),
            pltpu.VMEM(owned, BF16),
            pltpu.VMEM(owned, BF16),
            pltpu.VMEM((2, feature), F32),
            pltpu.VMEM((count, 2, feature), F32),
            pltpu.VMEM((8, feature), F32),
            pltpu.VMEM((8, feature), F32),
            pltpu.VMEM((8, entries), F32),
            pltpu.VMEM((8, entries), F32),
            pltpu.VMEM(halved, F32),
            pltpu.VMEM(halved, F32),
            pltpu.VMEM(halved, F32),
            pltpu.VMEM((16, rows_all), F32),
            pltpu.VMEM((feature, rows_all), F32),
            pltpu.SemaphoreType.DMA((7, count)),
            pltpu.SemaphoreType.DMA((7, count)),
            pltpu.SemaphoreType.DMA((4 + count,)),
            pltpu.SemaphoreType.DMA((4 + count,)),
            pltpu.SemaphoreType.DMA((12,)),
        ],
        compiler_params=pltpu.CompilerParams(
            collective_id=0, has_side_effects=True, vmem_limit_bytes=VMEM_LIMIT
        ),
    )(*in_hbm)
    in_grad, out_grad, gate_grad, tower_grad, table = pl.pallas_call(
        write_out,
        out_shape=[jax.ShapeDtypeStruct(value.shape, F32) for value in results],
        in_specs=[vmem] * 5,
        out_specs=[anywhere] * 5,
        scratch_shapes=[pltpu.SemaphoreType.DMA((20,))],
        compiler_params=pltpu.CompilerParams(vmem_limit_bytes=2**20),
    )(*[pltpu.with_memory_space_constraint(value, pltpu.VMEM) for value in results])
    return (in_grad[None], out_grad[None], gate_grad[None], tower_grad, table)


def solution(mesh):
    in_specs = (
        P(("expert", "dp"), None),
        P(("expert", "dp"), None),
        P(("expert", "dp"), None),
        P("expert", None, None),
        P("expert", None, None),
        P(),
        P(),
        P(),
        P(("expert", "dp")),
        P(("expert", "dp")),
        P(("expert", "dp")),
        P("expert", None),
    )
    out_specs = (
        P("expert", "dp", None),
        P("expert", "dp", None),
        P("expert", None, None),
        P(),
        P("expert", None),
    )
    return jax.shard_map(
        on_device, mesh=mesh, in_specs=in_specs, out_specs=out_specs, check_vma=False
    )
```

```python
import functools

import jax
import jax.numpy as jnp
from jax import lax
from jax.experimental import pallas as pl
from jax.experimental.pallas import tpu as pltpu
from jax.sharding import PartitionSpec as P

LOSS_SCALE = 32.0
STEP_SIZE = 0.25
F32, BF16 = jnp.float32, jnp.bfloat16
MESH = pl.DeviceIdType.MESH
VMEM_LIMIT = 47 * 2**20
SLOT_BASE = 4096


def mm(left, right, left_dim=1, right_dim=0):
    return lax.dot_general(
        left, right, (((left_dim,), (right_dim,)), ((), ())), preferred_element_type=F32
    )


def nt(left, right):
    return mm(left, right, 1, 1)


def halves(value):
    high = value.astype(BF16).astype(F32)
    return high, value - high


def stacked(value):
    return jnp.concatenate(halves(value), axis=0).astype(BF16)


def folded(value):
    half = value.shape[0] // 2
    return value[:half] + value[half:]


def sigmoid(value):
    return 0.5 * jnp.tanh(0.5 * value) + 0.5


def iota(shape, dim):
    return lax.broadcasted_iota(jnp.int32, shape, dim)


def one_hot(condition):
    return jnp.where(condition, 1.0, 0.0)


def lane_pack(pieces, width, lanes):
    lane = iota(pieces[0].shape, 1)
    rolled = [pltpu.roll(p, i * width % 128, 1) if i * width % 128 else p for i, p in enumerate(pieces)]
    parts = []
    for start in range(0, lanes, 128):
        total = jnp.zeros_like(pieces[0])
        for i, piece in enumerate(rolled):
            low, high = i * width - start, (i + 1) * width - start
            if high > 0 and low < 128:
                total = jnp.where((lane >= low) & (lane < high), piece, total)
        parts.append(total)
    return jnp.concatenate(parts, axis=1)


def kernel(
    sizes,
    pooled_hbm,
    routes_hbm,
    labels_hbm,
    in_hbm,
    out_hbm,
    gate_hbm,
    tower_hbm,
    bias_hbm,
    bag_rows_hbm,
    bag_sample_hbm,
    bag_weight_hbm,
    table_hbm,
    in_sum_ref,
    out_sum_ref,
    gate_sum_ref,
    tower_sum_ref,
    e_recv,
    e_other,
    pre_ref,
    table_ref,
    pooled_ref,
    routes_rows_ref,
    labels_ref,
    gate_ref,
    tower_ref,
    bias_ref,
    bag_rows_ref,
    bag_sample_ref,
    bag_weight_ref,
    in_ref,
    out_ref,
    turned_ref,
    proj_rows_ref,
    proj_cols_ref,
    act_ref,
    slope_ref,
    bag_place_ref,
    bag_acc,
    bag_weights,
    a_send,
    a_recv,
    m_send,
    m_recv,
    b_send,
    b_recv,
    d_send,
    d_recv,
    e_send,
    t_send,
    t_recv,
    s_send,
    s_recv,
    rows_mine,
    rows_other,
    hidden_mine,
    hidden_other,
    hidden_recv,
    rows_acc,
    back_acc,
    send_sem,
    recv_sem,
    dp_send,
    dp_recv,
    local_sem,
):
    count, cap, chunk, chunks, per_owner = sizes
    rows_all = count * cap
    tok_rows, feature = pooled_hbm.shape
    me, core = lax.axis_index("expert"), lax.axis_index("dp")
    other = 1 - core
    half = chunks // 2
    group = count // 2
    slots = group * cap
    blocks = slots // 128
    near = lax.div(me, group)
    far = 1 - near
    place_in = lax.rem(me, group)
    held = e_send.shape[1]
    entries = count * held

    def copy(phase, peer, sent, source, target, slot):
        return pltpu.make_async_remote_copy(
            src_ref=source,
            dst_ref=target,
            send_sem=send_sem.at[phase, sent],
            recv_sem=recv_sem.at[phase, slot],
            device_id={"expert": peer},
            device_id_type=MESH,
        )

    def onward(which, act):
        @pl.loop(1 if which == "near" else 0, group)
        def _(step):
            start = (near if which == "near" else far) * group
            act(start + lax.rem(place_in + step, group), near * group + step)

    def backward_from(which, low, high, act):
        @pl.loop(max(low, 1) if which == "near" else low, high)
        def _(position):
            start = (near if which == "near" else far) * group
            act(start + lax.rem(place_in - position + group, group), start + position)

    def everyone_on(act):
        onward("far", act)
        onward("near", act)

    def everyone_back(act):
        backward_from("near", 0, group, act)
        backward_from("far", 0, group, act)

    def rows_at(slot, size):
        return pl.ds(pl.multiple_of(slot * size, 8), size)

    def to_other(index, source, target):
        return pltpu.make_async_remote_copy(
            src_ref=source,
            dst_ref=target,
            send_sem=dp_send.at[index],
            recv_sem=dp_recv.at[index],
            device_id={"dp": other},
            device_id_type=MESH,
        )

    def a_copy(peer, slot):
        return copy(0, peer, peer, a_send.at[rows_at(peer, cap)], a_recv.at[rows_at(slot, cap)], slot)

    def m_copy(peer, slot):
        return copy(1, peer, peer, m_send.at[peer], m_recv.at[slot], slot)

    def b_copy(peer, slot, index):
        return copy(2 + index, peer, peer, b_send.at[index], b_recv.at[slot, index], slot)

    def d_copy(peer, position, slot):
        source = d_send.at[rows_at(position, cap)]
        return copy(4, peer, position, source, d_recv.at[rows_at(slot, cap)], slot)

    def e_copy(peer, slot):
        return copy(5, peer, peer, e_send.at[peer], e_recv.at[slot], slot)

    def t_copy(peer, slot):
        return copy(6, peer, peer, t_send, t_recv.at[slot], slot)

    barrier = pltpu.get_barrier_semaphore()

    @pl.loop(1, count)
    def _(step):
        pl.semaphore_signal(
            barrier, inc=1, device_id={"expert": lax.rem(me + step, count)}, device_id_type=MESH
        )

    pl.semaphore_signal(barrier, inc=1, device_id={"dp": other}, device_id_type=MESH)
    loads = [
        pltpu.make_async_copy(source, target, local_sem.at[index])
        for index, (source, target) in enumerate(
            (
                (routes_hbm, routes_rows_ref),
                (pooled_hbm, pooled_ref),
                (labels_hbm, labels_ref),
                (bag_rows_hbm, bag_rows_ref),
                (tower_hbm, tower_ref),
                (out_hbm, out_ref),
                (in_hbm, in_ref),
                (gate_hbm, gate_ref),
                (bias_hbm, bias_ref),
                (bag_sample_hbm, bag_sample_ref),
                (bag_weight_hbm, bag_weight_ref),
                (table_hbm, table_ref),
            )
        )
    ]
    for load in loads:
        load.start()
    loads[0].wait()

    first_row, second_row = routes_rows_ref[0:1, :], routes_rows_ref[1:2, :]
    first_map = one_hot(iota((count, tok_rows), 0) == first_row)
    second_map = one_hot(iota((count, tok_rows), 0) == second_row)
    above = one_hot(
        iota((tok_rows, tok_rows), 0) < iota((tok_rows, tok_rows), 1)
    ).astype(BF16)
    before = mm(jnp.concatenate([first_map, second_map], axis=0).astype(BF16), above)
    first_total = jnp.sum(first_map, axis=1, keepdims=True)
    first_rank = jnp.sum(first_map * before[:count], axis=0, keepdims=True).astype(jnp.int32)
    second_rank = jnp.sum(
        second_map * (before[count:] + first_total), axis=0, keepdims=True
    ).astype(jnp.int32)
    first_slot = first_rank + first_row * cap
    second_slot = second_rank + second_row * cap

    def fill_of(index):
        places = iota((slots, tok_rows), 0) + index * slots
        return one_hot((places == first_slot) | (places == second_slot)).astype(BF16)

    def send_half(index):
        rows = 0.5 * mm(fill_of(index), pooled_ref[...])
        a_send[rows_at(index, slots), :] = rows.astype(BF16)

    def far_start():
        onward("far", lambda peer, slot: a_copy(peer, slot).start())

    loads[1].wait()
    send_half(near)
    pl.semaphore_wait(barrier, count)
    onward("near", lambda peer, slot: a_copy(peer, slot).start())
    send_half(far)
    pl.when(core == 1)(far_start)
    a_recv[rows_at(near * group, cap), :] = a_send[rows_at(me, cap), :]
    for load in loads[2:5]:
        load.wait()

    lanes = iota((128, tok_rows), 0)
    first_at = one_hot(lanes == first_rank).astype(BF16)
    second_at = one_hot(lanes == second_rank).astype(BF16)
    label_code = 2 * labels_ref[0:1, :] + labels_ref[1:2, :] + 1

    def partner(own_map, row, rank):
        code = (4 * rank + label_code).astype(F32)
        return jnp.concatenate([own_map * row.astype(F32), own_map * code], axis=0).astype(BF16)

    told = nt(partner(first_map, second_row, second_rank), first_at) + nt(
        partner(second_map, first_row, first_rank), second_at
    )
    def position_at(expert):
        ahead = jnp.where(expert >= group, expert - group, expert) - place_in
        return jnp.where(ahead < 0, ahead + group, ahead)

    code = told[count:]
    ahead = (4 * cap * position_at(told[:count].astype(jnp.int32))).astype(F32)
    meta = jnp.where(code > 0.0, SLOT_BASE * told[:count] + code + ahead, 0.0)
    piece_lane = iota((1, 128), 1)
    for owner in range(count):
        start = owner * per_owner
        line = bag_rows_ref[start // 128 : start // 128 + 1, :].astype(F32)
        if start % 128:
            line = pltpu.roll(jnp.broadcast_to(line, (8, 128)), 128 - start % 128, 1)[0:1, :]
        m_send[owner, 0:1, :] = meta[owner : owner + 1, :]
        m_send[owner, 1:2, :] = jnp.where(piece_lane < per_owner, line, -1.0)
    m_recv[near * group] = m_send[me]

    feat_row = iota((8, feature), 0)
    tower_rows = jnp.where(
        feat_row == 0, tower_ref[0:1, :], jnp.where(feat_row == 1, tower_ref[1:2, :], 0.0)
    )
    tower_high, tower_low = halves(tower_rows)
    tower_high, tower_low = tower_high.astype(BF16), tower_low.astype(BF16)
    for load in loads[5:11]:
        load.wait()

    early = chunks // 2

    def project(step):
        span = pl.ds(pl.multiple_of(step * chunk, chunk), chunk)
        weights = out_ref[span, :]
        proj_rows_ref[step] = stacked(nt(tower_high, weights) + nt(tower_low, weights))
        cols = nt(weights, tower_high) + nt(weights, tower_low)
        proj_cols_ref[0, span, :] = jnp.broadcast_to(cols[:, 0:1], (chunk, 128))
        proj_cols_ref[1, span, :] = jnp.broadcast_to(cols[:, 1:2], (chunk, 128))
        turned_ref[step] = in_ref[span, :].T

    pl.loop(0, early)(project)
    pl.when(core == 0)(far_start)
    pl.loop(early, chunks)(project)
    rows_acc[...] = jnp.zeros_like(rows_acc)
    back_acc[...] = jnp.zeros_like(back_acc)

    def lanes_of(index, low, width):
        return pl.ds(pl.multiple_of(index * slots + low, 128), width)

    def forward(index, low, width, per):
        lane_span = lanes_of(index, low, width)

        @pl.loop(0, chunks // per)
        def _(outer):
            for inner in range(per):
                step = outer * per + inner
                span = pl.ds(pl.multiple_of(step * chunk, chunk), chunk)
                close = nt(in_ref[span, :], a_recv[lane_span, :])
                bend = jnp.tanh(close)
                twice = 1.0 + bend
                full = close * twice
                slope_ref[span, lane_span] = twice + full * (1.0 - bend)
                act = full.astype(BF16)
                act_ref[span, lane_span] = act
                rows_acc[:, lane_span] += mm(proj_rows_ref[step], act)

    def tell(index):
        dots = folded(rows_acc[:, lanes_of(index, 0, slots)])
        tile_row = iota((8, 128), 0)
        tile = jnp.zeros((8, 128), F32)
        for task in range(2):
            for block in range(blocks):
                piece = dots[task : task + 1, block * 128 : (block + 1) * 128]
                tile = jnp.where(tile_row == task * blocks + block, piece, tile)
        b_send[index] = tile
        b_recv[me, index] = tile
        everyone_on(lambda peer, slot: b_copy(peer, me, index).start())

    def a_wait(which, low, high):
        backward_from(which, low, high, lambda peer, slot: a_copy(peer, slot).wait_recv())

    a_wait("near", 0, group)
    forward(near, 0, slots, 1)
    a_wait("far", 0, group)
    everyone_on(lambda peer, slot: m_copy(peer, slot).start())
    tell(near)
    forward(far, 0, slots, 1)
    tell(far)

    everyone_back(lambda peer, slot: m_copy(peer, slot).wait_recv())
    pieces = [m_recv[source] for source in range(count)]
    told = jnp.concatenate(
        [lane_pack(pieces[i * group : (i + 1) * group], cap, slots)[0:1, :] for i in range(2)],
        axis=1,
    ).astype(jnp.int32)
    bag_lanes = -(-entries // 128) * 128
    rows_mine[...] = jnp.broadcast_to(
        lane_pack(pieces, held, bag_lanes)[1:2, :entries], rows_mine.shape
    )
    rows_copy = to_other(2, rows_mine, rows_other)
    rows_copy.start()
    valid = told > 0
    pair_expert = lax.shift_right_logical(told, 12)
    pair_code = jnp.bitwise_and(told, SLOT_BASE - 1) - 1
    pair_slot = lax.shift_right_logical(pair_code, 2)
    row_wide = iota((8, rows_all), 0)
    slot_labels = jnp.where(
        row_wide == 0,
        jnp.bitwise_and(lax.shift_right_logical(pair_code, 1), 1),
        jnp.bitwise_and(pair_code, 1),
    ).astype(F32)

    def dot_key(expert, slot):
        lane_of = one_hot(
            iota((128, slot.shape[1]), 0) == jnp.bitwise_and(slot, 127)
        ).astype(BF16)
        return lane_of, expert * 8 + lax.shift_right_logical(slot, 7)

    def look_up(tiles, key):
        lane_of, row_of_key = key
        found = folded(mm(tiles, lane_of))
        rows = iota(found.shape, 0)
        return [
            jnp.sum(
                jnp.where(rows == row_of_key + task * blocks, found, 0.0), axis=0, keepdims=True
            )
            for task in range(2)
        ]

    pair_key = dot_key(pair_expert, pair_slot)
    gates = [gate_ref[:, task, :] for task in range(2)]
    expert_row = iota((count, rows_all), 0)
    sign = one_hot(expert_row == me) - one_hot(expert_row == pair_expert)
    features_all = a_recv[...]
    slot_gate = jnp.zeros((8, rows_all), F32)
    for task in range(2):
        logits = nt(gates[task], features_all)
        slot_gate = jnp.where(
            row_wide == task, jnp.sum(sign * logits, axis=0, keepdims=True), slot_gate
        )
    own_gate = 0.5 * jnp.tanh(slot_gate) + 0.5
    pair_gate = 1.0 - own_gate
    gate_both = own_gate * pair_gate
    slot_bias = jnp.where(row_wide == 0, bias_ref[0], bias_ref[1])

    row_of = iota((8, tok_rows), 0)
    labels = jnp.where(row_of == 0, labels_ref[0:1, :], labels_ref[1:2, :]).astype(F32)
    bias = jnp.where(row_of == 0, bias_ref[0], bias_ref[1])
    signed = first_map - second_map
    gate_logit = jnp.zeros((8, tok_rows), F32)
    for task in range(2):
        logits = nt(gates[task], pooled_ref[...])
        gate_logit = jnp.where(
            row_of == task, jnp.sum(signed * logits, axis=0, keepdims=True), gate_logit
        )
    gate_first = sigmoid(gate_logit)
    gate_second = 1.0 - gate_first
    first_key = dot_key(first_row, first_rank + cap * position_at(first_row))
    second_key = dot_key(second_row, second_rank + cap * position_at(second_row))
    sample_wide = jnp.broadcast_to(bag_sample_ref[...].astype(F32), (8, entries))
    weight_wide = jnp.broadcast_to(bag_weight_ref[...], (8, entries))
    sample_col, weight_col = sample_wide.T[:, 0:1], weight_wide.T[:, 0:1]
    bag = one_hot(iota((entries, tok_rows), 1) == sample_col.astype(jnp.int32)).astype(BF16)
    for index in range(2):
        bag_place_ref[:, index * slots : (index + 1) * slots] = nt(bag, fill_of(index)).astype(BF16)

    for index in range(2):
        everyone_back(lambda peer, slot, index=index: b_copy(peer, peer, index).wait_recv())

    own_dot = folded(rows_acc[...])
    pair_dot = []
    for index in range(2):
        lane_span = slice(index * slots, (index + 1) * slots)
        tiles = stacked(b_recv[:, index].reshape(count * 8, 128))
        found = look_up(tiles, (pair_key[0][:, lane_span], pair_key[1][:, lane_span]))
        pair_dot.append(jnp.where(iota((8, slots), 0) == 0, found[0], found[1]))
    pair_dot = jnp.concatenate(pair_dot, axis=1)
    task_logit = own_gate * own_dot + pair_gate * pair_dot + slot_bias
    logit_grad = jnp.where(valid, LOSS_SCALE * (sigmoid(task_logit) - slot_labels), 0.0)
    gate_grad = pltpu.roll(logit_grad * (own_dot - pair_dot) * gate_both, 2, 0)
    coefs = jnp.where(
        row_wide < 2, own_gate * logit_grad, jnp.where(row_wide < 4, gate_grad, 0.0)
    )
    rows_acc[0:8, :] = coefs

    def backward(index, low, width, per):
        lane_span = lanes_of(index, low, width)
        coef_zero, coef_one = rows_acc[0:1, lane_span], rows_acc[1:2, lane_span]

        @pl.loop(0, chunks // per)
        def _(outer):
            for inner in range(per):
                step = outer * per + inner
                span = pl.ds(pl.multiple_of(step * chunk, chunk), chunk)
                zero, one = (
                    jnp.concatenate([proj_cols_ref[task, span, :]] * (width // 128), axis=1)
                    for task in range(2)
                )
                hidden_grad = zero * coef_zero + one * coef_one
                grad = (hidden_grad * slope_ref[span, lane_span]).astype(BF16)
                pre_ref[span, lane_span] = grad
                back_acc[:, lane_span] += mm(turned_ref[step], grad)

        d_send[lane_span, :] = (0.5 * back_acc[:, lane_span].T).astype(BF16)

    def d_start(which, low, high):
        backward_from(which, low, high, lambda peer, slot: d_copy(peer, slot, me).start())

    backward(far, 0, slots, 1)
    d_start("far", 0, group)
    backward(near, 0, slots, 1)
    d_start("near", 0, group)
    d_recv[rows_at(me, cap), :] = d_send[rows_at(near * group, cap), :]

    tiles = stacked(b_recv[:, near].reshape(count * 8, 128))

    def at_home(key):
        found = look_up(tiles, key)
        return jnp.where(row_of == 0, found[0], found[1])

    first_dot, second_dot = at_home(first_key), at_home(second_key)
    task_logit = gate_first * first_dot + gate_second * second_dot + bias
    logit_grad = LOSS_SCALE * (sigmoid(task_logit) - labels)
    first_grad = logit_grad * (first_dot - second_dot) * gate_first * gate_second
    gate_input = jnp.zeros((tok_rows, feature), F32)
    for task in range(2):
        high, low = halves(signed * first_grad[task : task + 1, :])
        gate_input += mm(high.astype(BF16), gates[task], 0, 0)
        gate_input += mm(low.astype(BF16), gates[task], 0, 0)
    high, low = halves(gate_input)
    bag_acc[...] = mm(bag, high.astype(BF16)) + mm(bag, low.astype(BF16))
    bag_weights[...] = jnp.broadcast_to(weight_col, (entries, 128))

    coef_rows = stacked(coefs)
    half_rows = half * chunk
    in_other = slope_ref.at[pl.ds(0, half_rows), pl.ds(0, feature)]
    in_mine = slope_ref.at[pl.ds(half_rows, half_rows), pl.ds(0, feature)]

    def hidden_chunk(step, target, slot):
        span = pl.ds(pl.multiple_of(step * chunk, chunk), chunk)
        hidden = folded(nt(coef_rows, act_ref[span, :]))
        target[slot] = hidden
        return folded(mm(stacked(hidden), out_ref[span, :]))

    def in_chunks(start, target):
        @pl.loop(0, half)
        def _(slot):
            span = pl.ds(pl.multiple_of((start + slot) * chunk, chunk), chunk)
            target[pl.ds(pl.multiple_of(slot * chunk, chunk), chunk), :] = mm(
                pre_ref[span, :], a_recv[...]
            )

    in_chunks(other * half, in_other)
    in_copy = to_other(0, in_other, in_sum_ref)
    in_copy.start()
    tower = jnp.zeros((8, feature), F32)
    for target, start in ((hidden_other, other * half), (hidden_mine, core * half)):
        tower = lax.fori_loop(
            0, half, lambda i, total, target=target, start=start: total + hidden_chunk(start + i, target, i), tower
        )
    hidden_copy = to_other(1, hidden_other, hidden_recv)
    hidden_copy.start()
    t_send[...] = tower[0:2]
    t_recv[me] = tower[0:2]

    everyone_on(lambda peer, slot: a_copy(peer, slot).wait_send())
    everyone_on(lambda peer, slot: m_copy(peer, slot).wait_send())
    for index in range(2):
        everyone_on(lambda peer, slot, index=index: b_copy(peer, me, index).wait_send())

    def bag_part(row_span, index):
        lane_span = pl.ds(pl.multiple_of(index * slots, 128), slots)
        return mm(bag_place_ref[row_span, lane_span], d_recv[rows_at(index, slots), :])

    def d_wait(which):
        backward_from(which, 0, group, lambda peer, slot: d_copy(peer, slot, peer).wait_recv())

    d_wait("near")
    bag_acc[...] += bag_part(pl.ds(0, entries), near)
    match_rows = entries // 2
    d_wait("far")
    everyone_on(lambda peer, slot: t_copy(peer, me).start())
    for which, index in (("far", far), ("near", near)):
        row_span = pl.ds(pl.multiple_of(index * match_rows, 8), match_rows)
        weights = jnp.concatenate([bag_weights[row_span, :]] * (feature // 128), axis=1)
        rows = weights * (bag_acc[row_span, :] + bag_part(row_span, far))
        e_send[pl.ds(index * group, group)] = rows.astype(BF16).reshape(group, held, feature)
        onward(which, lambda peer, slot: e_copy(peer, slot).start())

    def forwarded(slot, source):
        return to_other(4 + slot, source, e_other.at[slot])

    e_recv[near * group] = e_send[me]
    forwarded(near * group, e_send.at[me]).start()

    in_chunks(core * half, in_mine)
    gate = 2.0 * folded(mm(coef_rows, a_recv[...]))

    hidden_copy.wait()
    tower_three = jnp.concatenate(
        [tower_high.astype(F32), tower_low.astype(F32), tower_high.astype(F32)], axis=0
    ).astype(BF16)

    @pl.loop(0, half)
    def _(step):
        span = pl.ds(pl.multiple_of(step * chunk, chunk), chunk)
        high, low = halves(hidden_mine[step] + hidden_recv[step])
        three = jnp.concatenate([high, high, low], axis=0).astype(BF16)
        out_sum_ref[span, :] = mm(three, tower_three, 0, 0)

    in_copy.wait()

    @pl.loop(0, half)
    def _(step):
        span = pl.ds(pl.multiple_of(step * chunk, chunk), chunk)
        in_sum_ref[span, :] = in_sum_ref[span, :] + in_mine[span, :]

    for which in ("far", "near"):
        backward_from(which, 0, group, lambda peer, slot: d_copy(peer, slot, me).wait_send())
    rows_copy.wait()
    loads[11].wait()
    table_rows = table_ref.shape[0]
    part = table_rows // 4

    @pl.loop(0, 4)
    def _(step):
        numbers = (iota((part, entries), 0) + step * part).astype(F32)
        for index, row_numbers in enumerate((rows_mine, rows_other)):
            span = pl.ds(pl.multiple_of(index * table_rows + step * part, part), part)
            pre_ref[span, pl.ds(0, entries)] = jnp.where(
                numbers == row_numbers[0:1, :], STEP_SIZE, 0.0
            ).astype(BF16)

    def landed(peer, slot):
        e_copy(peer, slot).wait_recv()
        forwarded(slot, e_recv.at[slot]).start()

    def gather(index, values):
        half_entries = entries // 2
        lane_span = pl.ds(pl.multiple_of(near * half_entries, 128), half_entries)
        match = pre_ref[pl.ds(index * table_rows, table_rows), lane_span]
        sources = values[pl.ds(near * group, group)].reshape(half_entries, feature)
        table_ref[...] = table_ref[...] - mm(match, sources)

    backward_from("near", 0, group, landed)
    everyone_back(lambda peer, slot: t_copy(peer, peer).wait_recv())
    summed = t_recv[0]
    for source in range(1, count):
        summed = summed + t_recv[source]
    mine = jnp.concatenate([summed, gate[2:4], jnp.zeros((4, feature), F32)], axis=0)
    s_send[...] = mine
    small_copy = to_other(3, s_send, s_recv)
    small_copy.start()
    everyone_on(lambda peer, slot: t_copy(peer, me).wait_send())
    gather(0, e_recv)
    backward_from("far", 0, group, landed)
    everyone_on(lambda peer, slot: e_copy(peer, slot).wait_send())
    small_copy.wait()
    both = mine + s_recv[...]
    tower_sum_ref[...] = both[0:2]
    gate_sum_ref[...] = both[2:4]

    def crossed(peer, slot):
        forwarded(slot, e_recv.at[slot]).wait()

    crossed(me, near * group)
    backward_from("near", 0, group, crossed)
    gather(1, e_other)
    backward_from("far", 0, group, crossed)


def write_out(
    in_sum,
    out_sum,
    gate_sum,
    tower_sum,
    e_recv,
    e_other,
    matches,
    table_ref,
    in_out,
    out_out,
    gate_out,
    tower_out,
    table_out,
    sem,
):
    copies = []

    def start(source, target):
        copies.append(pltpu.make_async_copy(source, target, sem.at[len(copies)]))
        copies[-1].start()

    for source, target in ((in_sum, in_out), (out_sum, out_out)):
        rows = source.shape[0] // 4
        for part in range(4):
            span = pl.ds(part * rows, rows)
            start(source.at[span], target.at[span])
    start(gate_sum, gate_out)
    start(tower_sum, tower_out)
    group, held = e_recv.shape[0] // 2, e_recv.shape[1]
    half = group * held
    far = 1 - lax.div(lax.axis_index("expert"), group)
    lane_span = pl.ds(pl.multiple_of(far * half, 128), half)
    far_values = [
        values[pl.ds(far * group, group)].reshape(half, values.shape[2]) for values in (e_recv, e_other)
    ]
    table_rows = table_ref.shape[0]
    rows = table_rows // 4
    for part in range(4):
        span = pl.ds(part * rows, rows)
        total = table_ref[span, :]
        for index, values in enumerate(far_values):
            total = total - mm(matches[pl.ds(index * table_rows + part * rows, rows), lane_span], values)
        table_ref[span, :] = total
        start(table_ref.at[span], table_out.at[span])
    for copy in copies:
        copy.wait()


def on_device(
    pooled,
    routes,
    labels,
    in_weight,
    out_weight,
    gate_weight,
    tower_weight,
    tower_bias,
    bag_rows,
    bag_sample,
    bag_weight,
    row_table,
):
    count = lax.axis_size("expert")
    tok_rows, feature = pooled.shape
    tasks = tower_weight.shape[0]
    hidden = in_weight.shape[1]
    cap = -(-(3 * tok_rows // count) // 8) * 8
    rows_all = count * cap
    chunk = 1024 if rows_all * 1024 < 2**20 else 512
    chunks = hidden // chunk
    per_owner = bag_rows.shape[0] // count
    held = -(-per_owner // 8) * 8
    entries = count * held

    def bags(values, empty):
        if held == per_owner:
            return values
        return jnp.pad(
            values.reshape(count, per_owner), ((0, 0), (0, held - per_owner)), constant_values=empty
        )

    vmem = pl.BlockSpec(memory_space=pltpu.VMEM)
    anywhere = pl.BlockSpec(memory_space=pl.ANY)
    routed = (rows_all, feature)
    owned = (count, held, feature)
    half_rows = hidden // 2
    halved = (chunks // 2, 8, chunk)
    in_hbm = [
        pltpu.with_memory_space_constraint(value, pltpu.HBM)
        for value in (
            pooled,
            routes.T,
            labels.T,
            in_weight[0],
            out_weight[0],
            gate_weight,
            tower_weight,
            tower_bias,
            bag_rows.reshape(-1, 128),
            bags(bag_sample, -1).reshape(1, -1),
            bags(bag_weight, 0.0).reshape(1, -1),
            row_table,
        )
    ]
    results = pl.pallas_call(
        functools.partial(kernel, (count, cap, chunk, chunks, per_owner)),
        out_shape=(
            pltpu.VMEM((half_rows, feature), F32),
            pltpu.VMEM((half_rows, feature), F32),
            pltpu.VMEM((tasks, feature), F32),
            pltpu.VMEM((tasks, feature), F32),
            pltpu.VMEM(owned, BF16),
            pltpu.VMEM(owned, BF16),
            pltpu.VMEM((hidden, rows_all), BF16),
            pltpu.VMEM(row_table.shape, F32),
        ),
        in_specs=[anywhere] * 12,
        out_specs=(vmem,) * 8,
        scratch_shapes=[
            pltpu.VMEM(pooled.shape, BF16),
            pltpu.VMEM((2, tok_rows), jnp.int32),
            pltpu.VMEM((2, tok_rows), jnp.int32),
            pltpu.VMEM(gate_weight.shape, BF16),
            pltpu.VMEM(tower_weight.shape, F32),
            pltpu.SMEM(tower_bias.shape, F32),
            pltpu.VMEM((bag_rows.shape[0] // 128, 128), jnp.int32),
            pltpu.VMEM((1, entries), jnp.int32),
            pltpu.VMEM((1, entries), F32),
            pltpu.VMEM((hidden, feature), BF16),
            pltpu.VMEM((hidden, feature), BF16),
            pltpu.VMEM((chunks, feature, chunk), BF16),
            pltpu.VMEM((chunks, 16, chunk), BF16),
            pltpu.VMEM((2, hidden, 128), F32),
            pltpu.VMEM((hidden, rows_all), BF16),
            pltpu.VMEM((hidden, rows_all), F32),
            pltpu.VMEM((entries, rows_all), BF16),
            pltpu.VMEM((entries, feature), F32),
            pltpu.VMEM((entries, 128), F32),
            pltpu.VMEM(routed, BF16),
            pltpu.VMEM(routed, BF16),
            pltpu.VMEM((count, 2, 128), F32),
            pltpu.VMEM((count, 2, 128), F32),
            pltpu.VMEM((2, 8, 128), F32),
            pltpu.VMEM((count, 2, 8, 128), F32),
            pltpu.VMEM(routed, BF16),
            pltpu.VMEM(routed, BF16),
            pltpu.VMEM(owned, BF16),
            pltpu.VMEM((2, feature), F32),
            pltpu.VMEM((count, 2, feature), F32),
            pltpu.VMEM((8, feature), F32),
            pltpu.VMEM((8, feature), F32),
            pltpu.VMEM((8, entries), F32),
            pltpu.VMEM((8, entries), F32),
            pltpu.VMEM(halved, F32),
            pltpu.VMEM(halved, F32),
            pltpu.VMEM(halved, F32),
            pltpu.VMEM((16, rows_all), F32),
            pltpu.VMEM((feature, rows_all), F32),
            pltpu.SemaphoreType.DMA((7, count)),
            pltpu.SemaphoreType.DMA((7, count)),
            pltpu.SemaphoreType.DMA((4 + count,)),
            pltpu.SemaphoreType.DMA((4 + count,)),
            pltpu.SemaphoreType.DMA((12,)),
        ],
        compiler_params=pltpu.CompilerParams(
            collective_id=0, has_side_effects=True, vmem_limit_bytes=VMEM_LIMIT
        ),
    )(*in_hbm)
    in_grad, out_grad, gate_grad, tower_grad, table = pl.pallas_call(
        write_out,
        out_shape=[jax.ShapeDtypeStruct(value.shape, F32) for value in results[:4]]
        + [jax.ShapeDtypeStruct(row_table.shape, F32)],
        in_specs=[vmem] * 8,
        out_specs=[anywhere] * 5,
        scratch_shapes=[pltpu.SemaphoreType.DMA((16,))],
        compiler_params=pltpu.CompilerParams(vmem_limit_bytes=4 * 2**20),
    )(*[pltpu.with_memory_space_constraint(value, pltpu.VMEM) for value in results])
    return (in_grad[None], out_grad[None], gate_grad[None], tower_grad, table)


def solution(mesh):
    in_specs = (
        P(("expert", "dp"), None),
        P(("expert", "dp"), None),
        P(("expert", "dp"), None),
        P("expert", None, None),
        P("expert", None, None),
        P(),
        P(),
        P(),
        P(("expert", "dp")),
        P(("expert", "dp")),
        P(("expert", "dp")),
        P("expert", None),
    )
    out_specs = (
        P("expert", "dp", None),
        P("expert", "dp", None),
        P("expert", None, None),
        P(),
        P("expert", None),
    )
    return jax.shard_map(
        on_device, mesh=mesh, in_specs=in_specs, out_specs=out_specs, check_vma=False
    )
```

```python
import functools

import jax
import jax.numpy as jnp
from jax import lax
from jax.experimental import pallas as pl
from jax.experimental.pallas import tpu as pltpu
from jax.sharding import PartitionSpec as P

LOSS_SCALE = 32.0
STEP_SIZE = 0.25
F32, BF16 = jnp.float32, jnp.bfloat16
MESH = pl.DeviceIdType.MESH
VMEM_LIMIT = 47 * 2**20
SLOT_BASE = 4096


def mm(left, right, left_dim=1, right_dim=0):
    return lax.dot_general(
        left, right, (((left_dim,), (right_dim,)), ((), ())), preferred_element_type=F32
    )


def nt(left, right):
    return mm(left, right, 1, 1)


def halves(value):
    high = value.astype(BF16).astype(F32)
    return high, value - high


def stacked(value):
    return jnp.concatenate(halves(value), axis=0).astype(BF16)


def folded(value):
    half = value.shape[0] // 2
    return value[:half] + value[half:]


def sigmoid(value):
    return 0.5 * jnp.tanh(0.5 * value) + 0.5


def iota(shape, dim):
    return lax.broadcasted_iota(jnp.int32, shape, dim)


def one_hot(condition):
    return jnp.where(condition, 1.0, 0.0)


def lane_pack(pieces, width, lanes):
    lane = iota(pieces[0].shape, 1)
    rolled = [pltpu.roll(p, i * width % 128, 1) if i * width % 128 else p for i, p in enumerate(pieces)]
    parts = []
    for start in range(0, lanes, 128):
        total = jnp.zeros_like(pieces[0])
        for i, piece in enumerate(rolled):
            low, high = i * width - start, (i + 1) * width - start
            if high > 0 and low < 128:
                total = jnp.where((lane >= low) & (lane < high), piece, total)
        parts.append(total)
    return jnp.concatenate(parts, axis=1)


def kernel(
    sizes,
    pooled_hbm,
    routes_hbm,
    labels_hbm,
    in_hbm,
    out_hbm,
    gate_hbm,
    tower_hbm,
    bias_hbm,
    bag_rows_hbm,
    bag_sample_hbm,
    bag_weight_hbm,
    table_hbm,
    in_sum_ref,
    out_sum_ref,
    gate_sum_ref,
    tower_sum_ref,
    e_recv,
    e_other,
    pre_ref,
    table_ref,
    pooled_ref,
    routes_rows_ref,
    labels_ref,
    gate_ref,
    tower_ref,
    bias_ref,
    bag_rows_ref,
    bag_sample_ref,
    bag_weight_ref,
    in_ref,
    out_ref,
    turned_ref,
    proj_rows_ref,
    proj_cols_ref,
    act_ref,
    slope_ref,
    bag_place_ref,
    bag_acc,
    bag_weights,
    a_send,
    a_recv,
    m_send,
    m_recv,
    b_send,
    b_recv,
    d_send,
    d_recv,
    e_send,
    t_send,
    t_recv,
    s_send,
    s_recv,
    rows_mine,
    rows_other,
    hidden_mine,
    hidden_other,
    hidden_recv,
    rows_acc,
    back_acc,
    send_sem,
    recv_sem,
    dp_send,
    dp_recv,
    local_sem,
):
    count, cap, chunk, chunks, per_owner = sizes
    rows_all = count * cap
    tok_rows, feature = pooled_hbm.shape
    me, core = lax.axis_index("expert"), lax.axis_index("dp")
    other = 1 - core
    half = chunks // 2
    group = count // 2
    slots = group * cap
    blocks = slots // 128
    near = lax.div(me, group)
    far = 1 - near
    place_in = lax.rem(me, group)
    held = e_send.shape[1]
    entries = count * held

    def copy(phase, peer, sent, source, target, slot):
        return pltpu.make_async_remote_copy(
            src_ref=source,
            dst_ref=target,
            send_sem=send_sem.at[phase, sent],
            recv_sem=recv_sem.at[phase, slot],
            device_id={"expert": peer},
            device_id_type=MESH,
        )

    def onward(which, act):
        @pl.loop(1 if which == "near" else 0, group)
        def _(step):
            start = (near if which == "near" else far) * group
            act(start + lax.rem(place_in + step, group), near * group + step)

    def backward_from(which, low, high, act):
        @pl.loop(max(low, 1) if which == "near" else low, high)
        def _(position):
            start = (near if which == "near" else far) * group
            act(start + lax.rem(place_in - position + group, group), start + position)

    def everyone_on(act):
        onward("far", act)
        onward("near", act)

    def everyone_back(act):
        backward_from("near", 0, group, act)
        backward_from("far", 0, group, act)

    def rows_at(slot, size):
        return pl.ds(pl.multiple_of(slot * size, 8), size)

    def to_other(index, source, target):
        return pltpu.make_async_remote_copy(
            src_ref=source,
            dst_ref=target,
            send_sem=dp_send.at[index],
            recv_sem=dp_recv.at[index],
            device_id={"dp": other},
            device_id_type=MESH,
        )

    def a_copy(peer, slot):
        return copy(0, peer, peer, a_send.at[rows_at(peer, cap)], a_recv.at[rows_at(slot, cap)], slot)

    def m_copy(peer, slot):
        return copy(1, peer, peer, m_send.at[peer], m_recv.at[slot], slot)

    def b_copy(peer, slot, index):
        return copy(2 + index, peer, peer, b_send.at[index], b_recv.at[slot, index], slot)

    def d_copy(peer, position, slot):
        source = d_send.at[rows_at(position, cap)]
        return copy(4, peer, position, source, d_recv.at[rows_at(slot, cap)], slot)

    def e_copy(peer, slot):
        return copy(5, peer, peer, e_send.at[peer], e_recv.at[slot], slot)

    def t_copy(peer, slot):
        return copy(6, peer, peer, t_send, t_recv.at[slot], slot)

    barrier = pltpu.get_barrier_semaphore()

    @pl.loop(1, count)
    def _(step):
        pl.semaphore_signal(
            barrier, inc=1, device_id={"expert": lax.rem(me + step, count)}, device_id_type=MESH
        )

    pl.semaphore_signal(barrier, inc=1, device_id={"dp": other}, device_id_type=MESH)
    loads = [
        pltpu.make_async_copy(source, target, local_sem.at[index])
        for index, (source, target) in enumerate(
            (
                (routes_hbm, routes_rows_ref),
                (pooled_hbm, pooled_ref),
                (labels_hbm, labels_ref),
                (bag_rows_hbm, bag_rows_ref),
                (tower_hbm, tower_ref),
                (out_hbm, out_ref),
                (in_hbm, in_ref),
                (gate_hbm, gate_ref),
                (bias_hbm, bias_ref),
                (bag_sample_hbm, bag_sample_ref),
                (bag_weight_hbm, bag_weight_ref),
                (table_hbm, table_ref),
            )
        )
    ]
    for load in loads:
        load.start()
    loads[0].wait()

    first_row, second_row = routes_rows_ref[0:1, :], routes_rows_ref[1:2, :]
    first_map = one_hot(iota((count, tok_rows), 0) == first_row)
    second_map = one_hot(iota((count, tok_rows), 0) == second_row)
    above = one_hot(
        iota((tok_rows, tok_rows), 0) < iota((tok_rows, tok_rows), 1)
    ).astype(BF16)
    before = mm(jnp.concatenate([first_map, second_map], axis=0).astype(BF16), above)
    first_total = jnp.sum(first_map, axis=1, keepdims=True)
    first_rank = jnp.sum(first_map * before[:count], axis=0, keepdims=True).astype(jnp.int32)
    second_rank = jnp.sum(
        second_map * (before[count:] + first_total), axis=0, keepdims=True
    ).astype(jnp.int32)
    first_slot = first_rank + first_row * cap
    second_slot = second_rank + second_row * cap

    def fill_of(index):
        places = iota((slots, tok_rows), 0) + index * slots
        return one_hot((places == first_slot) | (places == second_slot)).astype(BF16)

    def send_half(index):
        rows = 0.5 * mm(fill_of(index), pooled_ref[...])
        a_send[rows_at(index, slots), :] = rows.astype(BF16)

    def far_start():
        onward("far", lambda peer, slot: a_copy(peer, slot).start())

    loads[1].wait()
    send_half(near)
    pl.semaphore_wait(barrier, count)
    onward("near", lambda peer, slot: a_copy(peer, slot).start())
    send_half(far)
    pl.when(core == 1)(far_start)
    a_recv[rows_at(near * group, cap), :] = a_send[rows_at(me, cap), :]
    for load in loads[2:5]:
        load.wait()

    lanes = iota((128, tok_rows), 0)
    first_at = one_hot(lanes == first_rank).astype(BF16)
    second_at = one_hot(lanes == second_rank).astype(BF16)
    label_code = 2 * labels_ref[0:1, :] + labels_ref[1:2, :] + 1

    def partner(own_map, row, rank):
        code = (4 * rank + label_code).astype(F32)
        return jnp.concatenate([own_map * row.astype(F32), own_map * code], axis=0).astype(BF16)

    told = nt(partner(first_map, second_row, second_rank), first_at) + nt(
        partner(second_map, first_row, first_rank), second_at
    )
    def position_at(expert):
        ahead = jnp.where(expert >= group, expert - group, expert) - place_in
        return jnp.where(ahead < 0, ahead + group, ahead)

    code = told[count:]
    ahead = (4 * cap * position_at(told[:count].astype(jnp.int32))).astype(F32)
    meta = jnp.where(code > 0.0, SLOT_BASE * told[:count] + code + ahead, 0.0)
    piece_lane = iota((1, 128), 1)
    for owner in range(count):
        start = owner * per_owner
        line = bag_rows_ref[start // 128 : start // 128 + 1, :].astype(F32)
        if start % 128:
            line = pltpu.roll(jnp.broadcast_to(line, (8, 128)), 128 - start % 128, 1)[0:1, :]
        m_send[owner, 0:1, :] = meta[owner : owner + 1, :]
        m_send[owner, 1:2, :] = jnp.where(piece_lane < per_owner, line, -1.0)
    m_recv[near * group] = m_send[me]

    feat_row = iota((8, feature), 0)
    tower_rows = jnp.where(
        feat_row == 0, tower_ref[0:1, :], jnp.where(feat_row == 1, tower_ref[1:2, :], 0.0)
    )
    tower_high, tower_low = halves(tower_rows)
    tower_two = stacked(tower_rows)
    wide_rows = iota((256, feature), 0) < 128
    wide_high, wide_low = (
        jnp.where(wide_rows, part[0:1, :], part[1:2, :]).astype(BF16)
        for part in (tower_high, tower_low)
    )
    tower_high, tower_low = tower_high.astype(BF16), tower_low.astype(BF16)
    for load in loads[5:11]:
        load.wait()

    early = chunks // 4

    def project(step):
        span = pl.ds(pl.multiple_of(step * chunk, chunk), chunk)
        weights = out_ref[span, :]
        proj_rows_ref[step] = stacked(folded(nt(tower_two, weights)))
        wide = nt(weights, wide_high) + nt(weights, wide_low)
        proj_cols_ref[0, span, :] = wide[:, :128]
        proj_cols_ref[1, span, :] = wide[:, 128:]
        turned_ref[step] = in_ref[span, :].T

    pl.loop(0, early)(project)
    pl.when(core == 0)(far_start)
    pl.loop(early, chunks)(project)
    rows_acc[...] = jnp.zeros_like(rows_acc)
    back_acc[...] = jnp.zeros_like(back_acc)

    def lanes_of(index, low, width):
        return pl.ds(pl.multiple_of(index * slots + low, 128), width)

    def forward(index, low, width, per):
        lane_span = lanes_of(index, low, width)

        @pl.loop(0, chunks // per)
        def _(outer):
            for inner in range(per):
                step = outer * per + inner
                span = pl.ds(pl.multiple_of(step * chunk, chunk), chunk)
                close = nt(in_ref[span, :], a_recv[lane_span, :])
                bend = jnp.tanh(close)
                twice = 1.0 + bend
                full = close * twice
                slope_ref[span, lane_span] = twice + full * (1.0 - bend)
                act = full.astype(BF16)
                act_ref[span, lane_span] = act
                rows_acc[:, lane_span] += mm(proj_rows_ref[step], act)

    def tell(index):
        dots = folded(rows_acc[:, lanes_of(index, 0, slots)])
        tile_row = iota((8, 128), 0)
        tile = jnp.zeros((8, 128), F32)
        for task in range(2):
            for block in range(blocks):
                piece = dots[task : task + 1, block * 128 : (block + 1) * 128]
                tile = jnp.where(tile_row == task * blocks + block, piece, tile)
        b_send[index] = tile
        b_recv[me, index] = tile
        everyone_on(lambda peer, slot: b_copy(peer, me, index).start())

    def a_wait(which, low, high):
        backward_from(which, low, high, lambda peer, slot: a_copy(peer, slot).wait_recv())

    a_wait("near", 0, group)
    forward(near, 0, slots, 2)
    a_wait("far", 0, group)
    everyone_on(lambda peer, slot: m_copy(peer, slot).start())
    tell(near)
    forward(far, 0, slots, 2)
    tell(far)

    everyone_back(lambda peer, slot: m_copy(peer, slot).wait_recv())
    pieces = [m_recv[source] for source in range(count)]
    told = jnp.concatenate(
        [lane_pack(pieces[i * group : (i + 1) * group], cap, slots)[0:1, :] for i in range(2)],
        axis=1,
    ).astype(jnp.int32)
    bag_lanes = -(-entries // 128) * 128
    rows_mine[...] = jnp.broadcast_to(
        lane_pack(pieces, held, bag_lanes)[1:2, :entries], rows_mine.shape
    )
    rows_copy = to_other(2, rows_mine, rows_other)
    rows_copy.start()
    valid = told > 0
    pair_expert = lax.shift_right_logical(told, 12)
    pair_code = jnp.bitwise_and(told, SLOT_BASE - 1) - 1
    pair_slot = lax.shift_right_logical(pair_code, 2)
    row_wide = iota((8, rows_all), 0)
    slot_labels = jnp.where(
        row_wide == 0,
        jnp.bitwise_and(lax.shift_right_logical(pair_code, 1), 1),
        jnp.bitwise_and(pair_code, 1),
    ).astype(F32)

    def dot_key(expert, slot):
        lane_of = one_hot(
            iota((128, slot.shape[1]), 0) == jnp.bitwise_and(slot, 127)
        ).astype(BF16)
        return lane_of, expert * 8 + lax.shift_right_logical(slot, 7)

    def look_up(tiles, key):
        lane_of, row_of_key = key
        found = folded(mm(tiles, lane_of))
        rows = iota(found.shape, 0)
        return [
            jnp.sum(
                jnp.where(rows == row_of_key + task * blocks, found, 0.0), axis=0, keepdims=True
            )
            for task in range(2)
        ]

    pair_key = dot_key(pair_expert, pair_slot)
    gates = [gate_ref[:, task, :] for task in range(2)]
    expert_row = iota((count, rows_all), 0)
    sign = one_hot(expert_row == me) - one_hot(expert_row == pair_expert)
    features_all = a_recv[...]
    slot_gate = jnp.zeros((8, rows_all), F32)
    for task in range(2):
        logits = nt(gates[task], features_all)
        slot_gate = jnp.where(
            row_wide == task, jnp.sum(sign * logits, axis=0, keepdims=True), slot_gate
        )
    own_gate = 0.5 * jnp.tanh(slot_gate) + 0.5
    pair_gate = 1.0 - own_gate
    gate_both = own_gate * pair_gate
    slot_bias = jnp.where(row_wide == 0, bias_ref[0], bias_ref[1])

    row_of = iota((8, tok_rows), 0)
    labels = jnp.where(row_of == 0, labels_ref[0:1, :], labels_ref[1:2, :]).astype(F32)
    bias = jnp.where(row_of == 0, bias_ref[0], bias_ref[1])
    signed = first_map - second_map
    gate_logit = jnp.zeros((8, tok_rows), F32)
    for task in range(2):
        logits = nt(gates[task], pooled_ref[...])
        gate_logit = jnp.where(
            row_of == task, jnp.sum(signed * logits, axis=0, keepdims=True), gate_logit
        )
    gate_first = sigmoid(gate_logit)
    gate_second = 1.0 - gate_first
    first_key = dot_key(first_row, first_rank + cap * position_at(first_row))
    second_key = dot_key(second_row, second_rank + cap * position_at(second_row))
    sample_wide = jnp.broadcast_to(bag_sample_ref[...].astype(F32), (8, entries))
    weight_wide = jnp.broadcast_to(bag_weight_ref[...], (8, entries))
    sample_col, weight_col = sample_wide.T[:, 0:1], weight_wide.T[:, 0:1]
    bag = one_hot(iota((entries, tok_rows), 1) == sample_col.astype(jnp.int32)).astype(BF16)
    for index in range(2):
        bag_place_ref[:, index * slots : (index + 1) * slots] = nt(bag, fill_of(index)).astype(BF16)

    for index in range(2):
        everyone_back(lambda peer, slot, index=index: b_copy(peer, peer, index).wait_recv())

    own_dot = folded(rows_acc[...])
    pair_dot = []
    for index in range(2):
        lane_span = slice(index * slots, (index + 1) * slots)
        tiles = stacked(b_recv[:, index].reshape(count * 8, 128))
        found = look_up(tiles, (pair_key[0][:, lane_span], pair_key[1][:, lane_span]))
        pair_dot.append(jnp.where(iota((8, slots), 0) == 0, found[0], found[1]))
    pair_dot = jnp.concatenate(pair_dot, axis=1)
    task_logit = own_gate * own_dot + pair_gate * pair_dot + slot_bias
    logit_grad = jnp.where(valid, LOSS_SCALE * (sigmoid(task_logit) - slot_labels), 0.0)
    gate_grad = pltpu.roll(logit_grad * (own_dot - pair_dot) * gate_both, 2, 0)
    coefs = jnp.where(
        row_wide < 2, own_gate * logit_grad, jnp.where(row_wide < 4, gate_grad, 0.0)
    )
    rows_acc[0:8, :] = coefs

    def backward(index, low, width, per):
        lane_span = lanes_of(index, low, width)
        coef_zero, coef_one = rows_acc[0:1, lane_span], rows_acc[1:2, lane_span]

        @pl.loop(0, chunks // per)
        def _(outer):
            for inner in range(per):
                step = outer * per + inner
                span = pl.ds(pl.multiple_of(step * chunk, chunk), chunk)
                zero, one = (
                    jnp.concatenate([proj_cols_ref[task, span, :]] * (width // 128), axis=1)
                    for task in range(2)
                )
                hidden_grad = zero * coef_zero + one * coef_one
                grad = (hidden_grad * slope_ref[span, lane_span]).astype(BF16)
                pre_ref[span, lane_span] = grad
                back_acc[:, lane_span] += mm(turned_ref[step], grad)

        d_send[lane_span, :] = (0.5 * back_acc[:, lane_span].T).astype(BF16)

    def d_start(which, low, high):
        backward_from(which, low, high, lambda peer, slot: d_copy(peer, slot, me).start())

    backward(far, 0, slots, 2)
    d_start("far", 0, group)
    backward(near, 0, slots, 2)
    d_start("near", 0, group)
    d_recv[rows_at(me, cap), :] = d_send[rows_at(near * group, cap), :]

    tiles = stacked(b_recv[:, near].reshape(count * 8, 128))

    def at_home(key):
        found = look_up(tiles, key)
        return jnp.where(row_of == 0, found[0], found[1])

    first_dot, second_dot = at_home(first_key), at_home(second_key)
    task_logit = gate_first * first_dot + gate_second * second_dot + bias
    logit_grad = LOSS_SCALE * (sigmoid(task_logit) - labels)
    first_grad = logit_grad * (first_dot - second_dot) * gate_first * gate_second
    gate_input = jnp.zeros((tok_rows, feature), F32)
    for task in range(2):
        high, low = halves(signed * first_grad[task : task + 1, :])
        gate_input += mm(high.astype(BF16), gates[task], 0, 0)
        gate_input += mm(low.astype(BF16), gates[task], 0, 0)
    high, low = halves(gate_input)
    bag_acc[...] = mm(bag, high.astype(BF16)) + mm(bag, low.astype(BF16))
    bag_weights[...] = jnp.broadcast_to(weight_col, (entries, 128))

    coef_rows = stacked(coefs)
    half_rows = half * chunk
    in_other = slope_ref.at[pl.ds(0, half_rows), pl.ds(0, feature)]
    in_mine = slope_ref.at[pl.ds(half_rows, half_rows), pl.ds(0, feature)]

    def hidden_chunk(step, target, slot):
        span = pl.ds(pl.multiple_of(step * chunk, chunk), chunk)
        hidden = folded(nt(coef_rows, act_ref[span, :]))
        target[slot] = hidden
        return folded(mm(stacked(hidden), out_ref[span, :]))

    def in_chunks(start, target):
        @pl.loop(0, half)
        def _(slot):
            span = pl.ds(pl.multiple_of((start + slot) * chunk, chunk), chunk)
            target[pl.ds(pl.multiple_of(slot * chunk, chunk), chunk), :] = mm(
                pre_ref[span, :], a_recv[...]
            )

    in_chunks(other * half, in_other)
    in_copy = to_other(0, in_other, in_sum_ref)
    in_copy.start()
    tower = jnp.zeros((8, feature), F32)
    for target, start in ((hidden_other, other * half), (hidden_mine, core * half)):
        tower = lax.fori_loop(
            0, half, lambda i, total, target=target, start=start: total + hidden_chunk(start + i, target, i), tower
        )
    hidden_copy = to_other(1, hidden_other, hidden_recv)
    hidden_copy.start()
    t_send[...] = tower[0:2]
    t_recv[me] = tower[0:2]

    everyone_on(lambda peer, slot: a_copy(peer, slot).wait_send())
    everyone_on(lambda peer, slot: m_copy(peer, slot).wait_send())
    for index in range(2):
        everyone_on(lambda peer, slot, index=index: b_copy(peer, me, index).wait_send())

    def bag_part(row_span, index):
        lane_span = pl.ds(pl.multiple_of(index * slots, 128), slots)
        return mm(bag_place_ref[row_span, lane_span], d_recv[rows_at(index, slots), :])

    def d_wait(which):
        backward_from(which, 0, group, lambda peer, slot: d_copy(peer, slot, peer).wait_recv())

    d_wait("near")
    bag_acc[...] += bag_part(pl.ds(0, entries), near)
    match_rows = entries // 2
    d_wait("far")
    everyone_on(lambda peer, slot: t_copy(peer, me).start())
    for which, index in (("far", far), ("near", near)):
        row_span = pl.ds(pl.multiple_of(index * match_rows, 8), match_rows)
        weights = jnp.concatenate([bag_weights[row_span, :]] * (feature // 128), axis=1)
        rows = weights * (bag_acc[row_span, :] + bag_part(row_span, far))
        e_send[pl.ds(index * group, group)] = rows.astype(BF16).reshape(group, held, feature)
        onward(which, lambda peer, slot: e_copy(peer, slot).start())

    def forwarded(slot, source):
        return to_other(4 + slot, source, e_other.at[slot])

    e_recv[near * group] = e_send[me]
    forwarded(near * group, e_send.at[me]).start()

    in_chunks(core * half, in_mine)
    gate = 2.0 * folded(mm(coef_rows, a_recv[...]))

    hidden_copy.wait()
    tower_three = jnp.concatenate(
        [tower_high.astype(F32), tower_low.astype(F32), tower_high.astype(F32)], axis=0
    ).astype(BF16)

    @pl.loop(0, half)
    def _(step):
        span = pl.ds(pl.multiple_of(step * chunk, chunk), chunk)
        high, low = halves(hidden_mine[step] + hidden_recv[step])
        three = jnp.concatenate([high, high, low], axis=0).astype(BF16)
        out_sum_ref[span, :] = mm(three, tower_three, 0, 0)

    in_copy.wait()

    @pl.loop(0, half)
    def _(step):
        span = pl.ds(pl.multiple_of(step * chunk, chunk), chunk)
        in_sum_ref[span, :] = in_sum_ref[span, :] + in_mine[span, :]

    for which in ("far", "near"):
        backward_from(which, 0, group, lambda peer, slot: d_copy(peer, slot, me).wait_send())
    rows_copy.wait()
    loads[11].wait()
    table_rows = table_ref.shape[0]
    part = table_rows // 4

    @pl.loop(0, 4)
    def _(step):
        numbers = (iota((part, entries), 0) + step * part).astype(F32)
        for index, row_numbers in enumerate((rows_mine, rows_other)):
            span = pl.ds(pl.multiple_of(index * table_rows + step * part, part), part)
            pre_ref[span, pl.ds(0, entries)] = jnp.where(
                numbers == row_numbers[0:1, :], STEP_SIZE, 0.0
            ).astype(BF16)

    def landed(peer, slot):
        e_copy(peer, slot).wait_recv()
        forwarded(slot, e_recv.at[slot]).start()

    def gather(index, values):
        half_entries = entries // 2
        lane_span = pl.ds(pl.multiple_of(near * half_entries, 128), half_entries)
        match = pre_ref[pl.ds(index * table_rows, table_rows), lane_span]
        sources = values[pl.ds(near * group, group)].reshape(half_entries, feature)
        table_ref[...] = table_ref[...] - mm(match, sources)

    backward_from("near", 0, group, landed)
    everyone_back(lambda peer, slot: t_copy(peer, peer).wait_recv())
    summed = t_recv[0]
    for source in range(1, count):
        summed = summed + t_recv[source]
    mine = jnp.concatenate([summed, gate[2:4], jnp.zeros((4, feature), F32)], axis=0)
    s_send[...] = mine
    small_copy = to_other(3, s_send, s_recv)
    small_copy.start()
    everyone_on(lambda peer, slot: t_copy(peer, me).wait_send())
    gather(0, e_recv)
    backward_from("far", 0, group, landed)
    everyone_on(lambda peer, slot: e_copy(peer, slot).wait_send())
    small_copy.wait()
    both = mine + s_recv[...]
    tower_sum_ref[...] = both[0:2]
    gate_sum_ref[...] = both[2:4]

    def crossed(peer, slot):
        forwarded(slot, e_recv.at[slot]).wait()

    crossed(me, near * group)
    backward_from("near", 0, group, crossed)
    gather(1, e_other)
    backward_from("far", 0, group, crossed)


def write_out(
    in_sum,
    out_sum,
    gate_sum,
    tower_sum,
    e_recv,
    e_other,
    matches,
    table_ref,
    in_out,
    out_out,
    gate_out,
    tower_out,
    table_out,
    sem,
):
    copies = []

    def start(source, target):
        copies.append(pltpu.make_async_copy(source, target, sem.at[len(copies)]))
        copies[-1].start()

    for source, target in ((in_sum, in_out), (out_sum, out_out)):
        rows = source.shape[0] // 4
        for part in range(4):
            span = pl.ds(part * rows, rows)
            start(source.at[span], target.at[span])
    start(gate_sum, gate_out)
    start(tower_sum, tower_out)
    group, held = e_recv.shape[0] // 2, e_recv.shape[1]
    half = group * held
    far = 1 - lax.div(lax.axis_index("expert"), group)
    lane_span = pl.ds(pl.multiple_of(far * half, 128), half)
    far_values = [
        values[pl.ds(far * group, group)].reshape(half, values.shape[2]) for values in (e_recv, e_other)
    ]
    table_rows = table_ref.shape[0]
    rows = table_rows // 4
    for part in range(4):
        span = pl.ds(part * rows, rows)
        total = table_ref[span, :]
        for index, values in enumerate(far_values):
            total = total - mm(matches[pl.ds(index * table_rows + part * rows, rows), lane_span], values)
        table_ref[span, :] = total
        start(table_ref.at[span], table_out.at[span])
    for copy in copies:
        copy.wait()


def on_device(
    pooled,
    routes,
    labels,
    in_weight,
    out_weight,
    gate_weight,
    tower_weight,
    tower_bias,
    bag_rows,
    bag_sample,
    bag_weight,
    row_table,
):
    count = lax.axis_size("expert")
    tok_rows, feature = pooled.shape
    tasks = tower_weight.shape[0]
    hidden = in_weight.shape[1]
    cap = -(-(3 * tok_rows // count) // 8) * 8
    rows_all = count * cap
    chunk = 1024 if rows_all * 1024 < 2**20 else 512
    chunks = hidden // chunk
    per_owner = bag_rows.shape[0] // count
    held = -(-per_owner // 8) * 8
    entries = count * held

    def bags(values, empty):
        if held == per_owner:
            return values
        return jnp.pad(
            values.reshape(count, per_owner), ((0, 0), (0, held - per_owner)), constant_values=empty
        )

    vmem = pl.BlockSpec(memory_space=pltpu.VMEM)
    anywhere = pl.BlockSpec(memory_space=pl.ANY)
    routed = (rows_all, feature)
    owned = (count, held, feature)
    half_rows = hidden // 2
    halved = (chunks // 2, 8, chunk)
    in_hbm = [
        pltpu.with_memory_space_constraint(value, pltpu.HBM)
        for value in (
            pooled,
            routes.T,
            labels.T,
            in_weight[0],
            out_weight[0],
            gate_weight,
            tower_weight,
            tower_bias,
            bag_rows.reshape(-1, 128),
            bags(bag_sample, -1).reshape(1, -1),
            bags(bag_weight, 0.0).reshape(1, -1),
            row_table,
        )
    ]
    results = pl.pallas_call(
        functools.partial(kernel, (count, cap, chunk, chunks, per_owner)),
        out_shape=(
            pltpu.VMEM((half_rows, feature), F32),
            pltpu.VMEM((half_rows, feature), F32),
            pltpu.VMEM((tasks, feature), F32),
            pltpu.VMEM((tasks, feature), F32),
            pltpu.VMEM(owned, BF16),
            pltpu.VMEM(owned, BF16),
            pltpu.VMEM((hidden, rows_all), BF16),
            pltpu.VMEM(row_table.shape, F32),
        ),
        in_specs=[anywhere] * 12,
        out_specs=(vmem,) * 8,
        scratch_shapes=[
            pltpu.VMEM(pooled.shape, BF16),
            pltpu.VMEM((2, tok_rows), jnp.int32),
            pltpu.VMEM((2, tok_rows), jnp.int32),
            pltpu.VMEM(gate_weight.shape, BF16),
            pltpu.VMEM(tower_weight.shape, F32),
            pltpu.SMEM(tower_bias.shape, F32),
            pltpu.VMEM((bag_rows.shape[0] // 128, 128), jnp.int32),
            pltpu.VMEM((1, entries), jnp.int32),
            pltpu.VMEM((1, entries), F32),
            pltpu.VMEM((hidden, feature), BF16),
            pltpu.VMEM((hidden, feature), BF16),
            pltpu.VMEM((chunks, feature, chunk), BF16),
            pltpu.VMEM((chunks, 16, chunk), BF16),
            pltpu.VMEM((2, hidden, 128), F32),
            pltpu.VMEM((hidden, rows_all), BF16),
            pltpu.VMEM((hidden, rows_all), F32),
            pltpu.VMEM((entries, rows_all), BF16),
            pltpu.VMEM((entries, feature), F32),
            pltpu.VMEM((entries, 128), F32),
            pltpu.VMEM(routed, BF16),
            pltpu.VMEM(routed, BF16),
            pltpu.VMEM((count, 2, 128), F32),
            pltpu.VMEM((count, 2, 128), F32),
            pltpu.VMEM((2, 8, 128), F32),
            pltpu.VMEM((count, 2, 8, 128), F32),
            pltpu.VMEM(routed, BF16),
            pltpu.VMEM(routed, BF16),
            pltpu.VMEM(owned, BF16),
            pltpu.VMEM((2, feature), F32),
            pltpu.VMEM((count, 2, feature), F32),
            pltpu.VMEM((8, feature), F32),
            pltpu.VMEM((8, feature), F32),
            pltpu.VMEM((8, entries), F32),
            pltpu.VMEM((8, entries), F32),
            pltpu.VMEM(halved, F32),
            pltpu.VMEM(halved, F32),
            pltpu.VMEM(halved, F32),
            pltpu.VMEM((16, rows_all), F32),
            pltpu.VMEM((feature, rows_all), F32),
            pltpu.SemaphoreType.DMA((7, count)),
            pltpu.SemaphoreType.DMA((7, count)),
            pltpu.SemaphoreType.DMA((4 + count,)),
            pltpu.SemaphoreType.DMA((4 + count,)),
            pltpu.SemaphoreType.DMA((12,)),
        ],
        compiler_params=pltpu.CompilerParams(
            collective_id=0, has_side_effects=True, vmem_limit_bytes=VMEM_LIMIT
        ),
    )(*in_hbm)
    in_grad, out_grad, gate_grad, tower_grad, table = pl.pallas_call(
        write_out,
        out_shape=[jax.ShapeDtypeStruct(value.shape, F32) for value in results[:4]]
        + [jax.ShapeDtypeStruct(row_table.shape, F32)],
        in_specs=[vmem] * 8,
        out_specs=[anywhere] * 5,
        scratch_shapes=[pltpu.SemaphoreType.DMA((16,))],
        compiler_params=pltpu.CompilerParams(vmem_limit_bytes=4 * 2**20),
    )(*[pltpu.with_memory_space_constraint(value, pltpu.VMEM) for value in results])
    return (in_grad[None], out_grad[None], gate_grad[None], tower_grad, table)


def solution(mesh):
    in_specs = (
        P(("expert", "dp"), None),
        P(("expert", "dp"), None),
        P(("expert", "dp"), None),
        P("expert", None, None),
        P("expert", None, None),
        P(),
        P(),
        P(),
        P(("expert", "dp")),
        P(("expert", "dp")),
        P(("expert", "dp")),
        P("expert", None),
    )
    out_specs = (
        P("expert", "dp", None),
        P("expert", "dp", None),
        P("expert", None, None),
        P(),
        P("expert", None),
    )
    return jax.shard_map(
        on_device, mesh=mesh, in_specs=in_specs, out_specs=out_specs, check_vma=False
    )
```

```python
import functools

import jax
import jax.numpy as jnp
from jax import lax
from jax.experimental import pallas as pl
from jax.experimental.pallas import tpu as pltpu
from jax.sharding import PartitionSpec as P

LOSS_SCALE = 32.0
STEP_SIZE = 0.25
F32, BF16 = jnp.float32, jnp.bfloat16
MESH = pl.DeviceIdType.MESH
VMEM_LIMIT = 47 * 2**20
SLOT_BASE = 4096


def mm(left, right, left_dim=1, right_dim=0):
    return lax.dot_general(
        left, right, (((left_dim,), (right_dim,)), ((), ())), preferred_element_type=F32
    )


def nt(left, right):
    return mm(left, right, 1, 1)


def halves(value):
    high = value.astype(BF16).astype(F32)
    return high, value - high


def stacked(value):
    return jnp.concatenate(halves(value), axis=0).astype(BF16)


def folded(value):
    half = value.shape[0] // 2
    return value[:half] + value[half:]


def sigmoid(value):
    return 0.5 * jnp.tanh(0.5 * value) + 0.5


def iota(shape, dim):
    return lax.broadcasted_iota(jnp.int32, shape, dim)


def one_hot(condition):
    return jnp.where(condition, 1.0, 0.0)


def lane_pack(pieces, width, lanes):
    lane = iota(pieces[0].shape, 1)
    rolled = [pltpu.roll(p, i * width % 128, 1) if i * width % 128 else p for i, p in enumerate(pieces)]
    parts = []
    for start in range(0, lanes, 128):
        total = jnp.zeros_like(pieces[0])
        for i, piece in enumerate(rolled):
            low, high = i * width - start, (i + 1) * width - start
            if high > 0 and low < 128:
                total = jnp.where((lane >= low) & (lane < high), piece, total)
        parts.append(total)
    return jnp.concatenate(parts, axis=1)


def kernel(
    sizes,
    pooled_hbm,
    routes_hbm,
    labels_hbm,
    in_hbm,
    out_hbm,
    gate_hbm,
    tower_hbm,
    bias_hbm,
    bag_rows_hbm,
    bag_sample_hbm,
    bag_weight_hbm,
    table_hbm,
    in_sum_ref,
    out_sum_ref,
    gate_sum_ref,
    tower_sum_ref,
    e_recv,
    e_other,
    pre_ref,
    table_ref,
    pooled_ref,
    routes_rows_ref,
    labels_ref,
    gate_ref,
    tower_ref,
    bias_ref,
    bag_rows_ref,
    bag_sample_ref,
    bag_weight_ref,
    in_ref,
    out_ref,
    turned_ref,
    proj_rows_ref,
    proj_cols_ref,
    act_ref,
    slope_ref,
    bag_place_ref,
    bag_acc,
    bag_weights,
    a_send,
    a_recv,
    m_send,
    m_recv,
    b_send,
    b_recv,
    d_send,
    d_recv,
    e_send,
    t_send,
    t_recv,
    s_send,
    s_recv,
    rows_mine,
    rows_other,
    hidden_mine,
    hidden_other,
    hidden_recv,
    rows_acc,
    back_acc,
    send_sem,
    recv_sem,
    dp_send,
    dp_recv,
    local_sem,
):
    count, cap, chunk, chunks, per_owner = sizes
    rows_all = count * cap
    tok_rows, feature = pooled_hbm.shape
    me, core = lax.axis_index("expert"), lax.axis_index("dp")
    other = 1 - core
    half = chunks // 2
    group = count // 2
    slots = group * cap
    blocks = slots // 128
    near = lax.div(me, group)
    far = 1 - near
    place_in = lax.rem(me, group)
    held = e_send.shape[1]
    entries = count * held

    def copy(phase, peer, sent, source, target, slot):
        return pltpu.make_async_remote_copy(
            src_ref=source,
            dst_ref=target,
            send_sem=send_sem.at[phase, sent],
            recv_sem=recv_sem.at[phase, slot],
            device_id={"expert": peer},
            device_id_type=MESH,
        )

    def onward(which, act):
        @pl.loop(1 if which == "near" else 0, group)
        def _(step):
            start = (near if which == "near" else far) * group
            act(start + lax.rem(place_in + step, group), near * group + step)

    def backward_from(which, low, high, act):
        @pl.loop(max(low, 1) if which == "near" else low, high)
        def _(position):
            start = (near if which == "near" else far) * group
            act(start + lax.rem(place_in - position + group, group), start + position)

    def everyone_on(act):
        onward("far", act)
        onward("near", act)

    def everyone_back(act):
        backward_from("near", 0, group, act)
        backward_from("far", 0, group, act)

    def rows_at(slot, size):
        return pl.ds(pl.multiple_of(slot * size, 8), size)

    def to_other(index, source, target):
        return pltpu.make_async_remote_copy(
            src_ref=source,
            dst_ref=target,
            send_sem=dp_send.at[index],
            recv_sem=dp_recv.at[index],
            device_id={"dp": other},
            device_id_type=MESH,
        )

    def a_copy(peer, slot):
        return copy(0, peer, peer, a_send.at[rows_at(peer, cap)], a_recv.at[rows_at(slot, cap)], slot)

    def m_copy(peer, slot):
        return copy(1, peer, peer, m_send.at[peer], m_recv.at[slot], slot)

    def b_copy(peer, slot, index):
        return copy(2 + index, peer, peer, b_send.at[index], b_recv.at[slot, index], slot)

    def d_copy(peer, position, slot):
        source = d_send.at[rows_at(position, cap)]
        return copy(4, peer, position, source, d_recv.at[rows_at(slot, cap)], slot)

    def e_copy(peer, slot):
        return copy(5, peer, peer, e_send.at[peer], e_recv.at[slot], slot)

    def t_copy(peer, slot):
        return copy(6, peer, peer, t_send, t_recv.at[slot], slot)

    barrier = pltpu.get_barrier_semaphore()

    @pl.loop(1, count)
    def _(step):
        pl.semaphore_signal(
            barrier, inc=1, device_id={"expert": lax.rem(me + step, count)}, device_id_type=MESH
        )

    pl.semaphore_signal(barrier, inc=1, device_id={"dp": other}, device_id_type=MESH)
    loads = [
        pltpu.make_async_copy(source, target, local_sem.at[index])
        for index, (source, target) in enumerate(
            (
                (routes_hbm, routes_rows_ref),
                (pooled_hbm, pooled_ref),
                (labels_hbm, labels_ref),
                (bag_rows_hbm, bag_rows_ref),
                (tower_hbm, tower_ref),
                (out_hbm, out_ref),
                (in_hbm, in_ref),
                (gate_hbm, gate_ref),
                (bias_hbm, bias_ref),
                (bag_sample_hbm, bag_sample_ref),
                (bag_weight_hbm, bag_weight_ref),
                (table_hbm, table_ref),
            )
        )
    ]
    for load in loads:
        load.start()
    loads[0].wait()

    first_row, second_row = routes_rows_ref[0:1, :], routes_rows_ref[1:2, :]
    first_map = one_hot(iota((count, tok_rows), 0) == first_row)
    second_map = one_hot(iota((count, tok_rows), 0) == second_row)
    above = one_hot(
        iota((tok_rows, tok_rows), 0) < iota((tok_rows, tok_rows), 1)
    ).astype(BF16)
    before = mm(jnp.concatenate([first_map, second_map], axis=0).astype(BF16), above)
    first_total = jnp.sum(first_map, axis=1, keepdims=True)
    first_rank = jnp.sum(first_map * before[:count], axis=0, keepdims=True).astype(jnp.int32)
    second_rank = jnp.sum(
        second_map * (before[count:] + first_total), axis=0, keepdims=True
    ).astype(jnp.int32)
    first_slot = first_rank + first_row * cap
    second_slot = second_rank + second_row * cap

    def fill_of(index):
        places = iota((slots, tok_rows), 0) + index * slots
        return one_hot((places == first_slot) | (places == second_slot)).astype(BF16)

    def send_half(index):
        rows = 0.5 * mm(fill_of(index), pooled_ref[...])
        a_send[rows_at(index, slots), :] = rows.astype(BF16)

    def far_start():
        onward("far", lambda peer, slot: a_copy(peer, slot).start())

    loads[1].wait()
    send_half(near)
    pl.semaphore_wait(barrier, count)
    onward("near", lambda peer, slot: a_copy(peer, slot).start())
    send_half(far)
    pl.when(core == 1)(far_start)
    a_recv[rows_at(near * group, cap), :] = a_send[rows_at(me, cap), :]
    for load in loads[2:5]:
        load.wait()

    lanes = iota((128, tok_rows), 0)
    first_at = one_hot(lanes == first_rank).astype(BF16)
    second_at = one_hot(lanes == second_rank).astype(BF16)
    label_code = 2 * labels_ref[0:1, :] + labels_ref[1:2, :] + 1

    def partner(own_map, row, rank):
        code = (4 * rank + label_code).astype(F32)
        return jnp.concatenate([own_map * row.astype(F32), own_map * code], axis=0).astype(BF16)

    told = nt(partner(first_map, second_row, second_rank), first_at) + nt(
        partner(second_map, first_row, first_rank), second_at
    )
    def position_at(expert):
        ahead = jnp.where(expert >= group, expert - group, expert) - place_in
        return jnp.where(ahead < 0, ahead + group, ahead)

    code = told[count:]
    ahead = (4 * cap * position_at(told[:count].astype(jnp.int32))).astype(F32)
    meta = jnp.where(code > 0.0, SLOT_BASE * told[:count] + code + ahead, 0.0)
    piece_lane = iota((1, 128), 1)
    for owner in range(count):
        start = owner * per_owner
        line = bag_rows_ref[start // 128 : start // 128 + 1, :].astype(F32)
        if start % 128:
            line = pltpu.roll(jnp.broadcast_to(line, (8, 128)), 128 - start % 128, 1)[0:1, :]
        m_send[owner, 0:1, :] = meta[owner : owner + 1, :]
        m_send[owner, 1:2, :] = jnp.where(piece_lane < per_owner, line, -1.0)
    m_recv[near * group] = m_send[me]

    feat_row = iota((8, feature), 0)
    tower_rows = jnp.where(
        feat_row == 0, tower_ref[0:1, :], jnp.where(feat_row == 1, tower_ref[1:2, :], 0.0)
    )
    tower_high, tower_low = halves(tower_rows)
    tower_two = stacked(tower_rows)
    wide_rows = iota((256, feature), 0) < 128
    wide_high, wide_low = (
        jnp.where(wide_rows, part[0:1, :], part[1:2, :]).astype(BF16)
        for part in (tower_high, tower_low)
    )
    tower_high, tower_low = tower_high.astype(BF16), tower_low.astype(BF16)
    for load in loads[5:11]:
        load.wait()

    early = chunks // 4

    def project(step):
        span = pl.ds(pl.multiple_of(step * chunk, chunk), chunk)
        weights = out_ref[span, :]
        proj_rows_ref[step] = stacked(folded(nt(tower_two, weights)))
        wide = nt(weights, wide_high) + nt(weights, wide_low)
        proj_cols_ref[0, span, :] = wide[:, :128]
        proj_cols_ref[1, span, :] = wide[:, 128:]
        turned_ref[step] = in_ref[span, :].T

    pl.loop(0, early)(project)
    pl.when(core == 0)(far_start)
    pl.loop(early, chunks)(project)
    rows_acc[...] = jnp.zeros_like(rows_acc)
    back_acc[...] = jnp.zeros_like(back_acc)

    def lanes_of(index, low, width):
        return pl.ds(pl.multiple_of(index * slots + low, 128), width)

    def forward(index, low, width, per):
        lane_span = lanes_of(index, low, width)

        @pl.loop(0, chunks // per)
        def _(outer):
            for inner in range(per):
                step = outer * per + inner
                span = pl.ds(pl.multiple_of(step * chunk, chunk), chunk)
                close = nt(in_ref[span, :], a_recv[lane_span, :])
                bend = jnp.tanh(close)
                twice = 1.0 + bend
                full = close * twice
                slope_ref[span, lane_span] = twice + full * (1.0 - bend)
                act = full.astype(BF16)
                act_ref[span, lane_span] = act
                rows_acc[:, lane_span] += mm(proj_rows_ref[step], act)

    def tell(index):
        dots = folded(rows_acc[:, lanes_of(index, 0, slots)])
        tile_row = iota((8, 128), 0)
        tile = jnp.zeros((8, 128), F32)
        for task in range(2):
            for block in range(blocks):
                piece = dots[task : task + 1, block * 128 : (block + 1) * 128]
                tile = jnp.where(tile_row == task * blocks + block, piece, tile)
        b_send[index] = tile
        b_recv[me, index] = tile
        everyone_on(lambda peer, slot: b_copy(peer, me, index).start())

    def a_wait(which, low, high):
        backward_from(which, low, high, lambda peer, slot: a_copy(peer, slot).wait_recv())

    a_wait("near", 0, group)
    forward(near, 0, slots, 2)
    a_wait("far", 0, group)
    everyone_on(lambda peer, slot: m_copy(peer, slot).start())
    tell(near)
    forward(far, 0, slots, 2)
    tell(far)

    everyone_back(lambda peer, slot: m_copy(peer, slot).wait_recv())
    pieces = [m_recv[source] for source in range(count)]
    told = jnp.concatenate(
        [lane_pack(pieces[i * group : (i + 1) * group], cap, slots)[0:1, :] for i in range(2)],
        axis=1,
    ).astype(jnp.int32)
    bag_lanes = -(-entries // 128) * 128
    rows_mine[...] = jnp.broadcast_to(
        lane_pack(pieces, held, bag_lanes)[1:2, :entries], rows_mine.shape
    )
    rows_copy = to_other(2, rows_mine, rows_other)
    rows_copy.start()
    valid = told > 0
    pair_expert = lax.shift_right_logical(told, 12)
    pair_code = jnp.bitwise_and(told, SLOT_BASE - 1) - 1
    pair_slot = lax.shift_right_logical(pair_code, 2)
    row_wide = iota((8, rows_all), 0)
    slot_labels = jnp.where(
        row_wide == 0,
        jnp.bitwise_and(lax.shift_right_logical(pair_code, 1), 1),
        jnp.bitwise_and(pair_code, 1),
    ).astype(F32)

    def dot_key(expert, slot):
        lane_of = one_hot(
            iota((128, slot.shape[1]), 0) == jnp.bitwise_and(slot, 127)
        ).astype(BF16)
        return lane_of, expert * 8 + lax.shift_right_logical(slot, 7)

    def look_up(tiles, key):
        lane_of, row_of_key = key
        found = folded(mm(tiles, lane_of))
        rows = iota(found.shape, 0)
        return [
            jnp.sum(
                jnp.where(rows == row_of_key + task * blocks, found, 0.0), axis=0, keepdims=True
            )
            for task in range(2)
        ]

    pair_key = dot_key(pair_expert, pair_slot)
    gates = [gate_ref[:, task, :] for task in range(2)]
    expert_row = iota((count, rows_all), 0)
    sign = one_hot(expert_row == me) - one_hot(expert_row == pair_expert)
    features_all = a_recv[...]
    slot_gate = jnp.zeros((8, rows_all), F32)
    for task in range(2):
        logits = nt(gates[task], features_all)
        slot_gate = jnp.where(
            row_wide == task, jnp.sum(sign * logits, axis=0, keepdims=True), slot_gate
        )
    own_gate = 0.5 * jnp.tanh(slot_gate) + 0.5
    pair_gate = 1.0 - own_gate
    gate_both = own_gate * pair_gate
    slot_bias = jnp.where(row_wide == 0, bias_ref[0], bias_ref[1])

    row_of = iota((8, tok_rows), 0)
    labels = jnp.where(row_of == 0, labels_ref[0:1, :], labels_ref[1:2, :]).astype(F32)
    bias = jnp.where(row_of == 0, bias_ref[0], bias_ref[1])
    signed = first_map - second_map
    gate_logit = jnp.zeros((8, tok_rows), F32)
    for task in range(2):
        logits = nt(gates[task], pooled_ref[...])
        gate_logit = jnp.where(
            row_of == task, jnp.sum(signed * logits, axis=0, keepdims=True), gate_logit
        )
    gate_first = sigmoid(gate_logit)
    gate_second = 1.0 - gate_first
    first_key = dot_key(first_row, first_rank + cap * position_at(first_row))
    second_key = dot_key(second_row, second_rank + cap * position_at(second_row))
    sample_wide = jnp.broadcast_to(bag_sample_ref[...].astype(F32), (8, entries))
    weight_wide = jnp.broadcast_to(bag_weight_ref[...], (8, entries))
    sample_col, weight_col = sample_wide.T[:, 0:1], weight_wide.T[:, 0:1]
    bag = one_hot(iota((entries, tok_rows), 1) == sample_col.astype(jnp.int32)).astype(BF16)
    for index in range(2):
        bag_place_ref[:, index * slots : (index + 1) * slots] = nt(bag, fill_of(index)).astype(BF16)

    for index in range(2):
        everyone_back(lambda peer, slot, index=index: b_copy(peer, peer, index).wait_recv())

    own_dot = folded(rows_acc[...])
    pair_dot = []
    for index in range(2):
        lane_span = slice(index * slots, (index + 1) * slots)
        tiles = stacked(b_recv[:, index].reshape(count * 8, 128))
        found = look_up(tiles, (pair_key[0][:, lane_span], pair_key[1][:, lane_span]))
        pair_dot.append(jnp.where(iota((8, slots), 0) == 0, found[0], found[1]))
    pair_dot = jnp.concatenate(pair_dot, axis=1)
    task_logit = own_gate * own_dot + pair_gate * pair_dot + slot_bias
    logit_grad = jnp.where(valid, LOSS_SCALE * (sigmoid(task_logit) - slot_labels), 0.0)
    gate_grad = pltpu.roll(logit_grad * (own_dot - pair_dot) * gate_both, 2, 0)
    coefs = jnp.where(
        row_wide < 2, own_gate * logit_grad, jnp.where(row_wide < 4, gate_grad, 0.0)
    )
    rows_acc[0:8, :] = coefs

    def backward(index, low, width, per):
        lane_span = lanes_of(index, low, width)
        coef_zero, coef_one = rows_acc[0:1, lane_span], rows_acc[1:2, lane_span]

        @pl.loop(0, chunks // per)
        def _(outer):
            for inner in range(per):
                step = outer * per + inner
                span = pl.ds(pl.multiple_of(step * chunk, chunk), chunk)
                zero, one = (
                    jnp.concatenate([proj_cols_ref[task, span, :]] * (width // 128), axis=1)
                    for task in range(2)
                )
                hidden_grad = zero * coef_zero + one * coef_one
                grad = (hidden_grad * slope_ref[span, lane_span]).astype(BF16)
                pre_ref[span, lane_span] = grad
                back_acc[:, lane_span] += mm(turned_ref[step], grad)

        d_send[lane_span, :] = (0.5 * back_acc[:, lane_span].T).astype(BF16)

    def d_start(which, low, high):
        backward_from(which, low, high, lambda peer, slot: d_copy(peer, slot, me).start())

    backward(far, 0, slots, 2)
    d_start("far", 0, group)
    backward(near, 0, slots, 2)
    d_start("near", 0, group)
    d_recv[rows_at(me, cap), :] = d_send[rows_at(near * group, cap), :]

    tiles = stacked(b_recv[:, near].reshape(count * 8, 128))

    def at_home(key):
        found = look_up(tiles, key)
        return jnp.where(row_of == 0, found[0], found[1])

    first_dot, second_dot = at_home(first_key), at_home(second_key)
    task_logit = gate_first * first_dot + gate_second * second_dot + bias
    logit_grad = LOSS_SCALE * (sigmoid(task_logit) - labels)
    first_grad = logit_grad * (first_dot - second_dot) * gate_first * gate_second
    gate_input = jnp.zeros((tok_rows, feature), F32)
    for task in range(2):
        high, low = halves(signed * first_grad[task : task + 1, :])
        gate_input += mm(high.astype(BF16), gates[task], 0, 0)
        gate_input += mm(low.astype(BF16), gates[task], 0, 0)
    high, low = halves(gate_input)
    bag_acc[...] = mm(bag, high.astype(BF16)) + mm(bag, low.astype(BF16))
    bag_weights[...] = jnp.broadcast_to(weight_col, (entries, 128))

    coef_rows = stacked(coefs)
    half_rows = half * chunk
    in_other = slope_ref.at[pl.ds(0, half_rows), pl.ds(0, feature)]
    in_mine = slope_ref.at[pl.ds(half_rows, half_rows), pl.ds(0, feature)]

    def hidden_chunk(step, target, slot):
        span = pl.ds(pl.multiple_of(step * chunk, chunk), chunk)
        hidden = folded(nt(coef_rows, act_ref[span, :]))
        target[slot] = hidden
        return folded(mm(stacked(hidden), out_ref[span, :]))

    def in_chunks(start, target):
        @pl.loop(0, half)
        def _(slot):
            span = pl.ds(pl.multiple_of((start + slot) * chunk, chunk), chunk)
            target[pl.ds(pl.multiple_of(slot * chunk, chunk), chunk), :] = mm(
                pre_ref[span, :], a_recv[...]
            )

    in_chunks(other * half, in_other)
    in_copy = to_other(0, in_other, in_sum_ref)
    in_copy.start()
    tower = jnp.zeros((8, feature), F32)
    for target, start in ((hidden_other, other * half), (hidden_mine, core * half)):
        tower = lax.fori_loop(
            0, half, lambda i, total, target=target, start=start: total + hidden_chunk(start + i, target, i), tower
        )
    hidden_copy = to_other(1, hidden_other, hidden_recv)
    hidden_copy.start()
    t_send[...] = tower[0:2]
    t_recv[me] = tower[0:2]

    def drain():
        everyone_on(lambda peer, slot: a_copy(peer, slot).wait_send())
        everyone_on(lambda peer, slot: m_copy(peer, slot).wait_send())
        for index in range(2):
            everyone_on(lambda peer, slot, index=index: b_copy(peer, me, index).wait_send())

    pl.when(core == 1)(drain)

    def bag_part(row_span, index):
        lane_span = pl.ds(pl.multiple_of(index * slots, 128), slots)
        return mm(bag_place_ref[row_span, lane_span], d_recv[rows_at(index, slots), :])

    def d_wait(which):
        backward_from(which, 0, group, lambda peer, slot: d_copy(peer, slot, peer).wait_recv())

    d_wait("near")
    bag_acc[...] += bag_part(pl.ds(0, entries), near)
    match_rows = entries // 2
    d_wait("far")
    everyone_on(lambda peer, slot: t_copy(peer, me).start())
    for which, index in (("far", far), ("near", near)):
        row_span = pl.ds(pl.multiple_of(index * match_rows, 8), match_rows)
        weights = jnp.concatenate([bag_weights[row_span, :]] * (feature // 128), axis=1)
        rows = weights * (bag_acc[row_span, :] + bag_part(row_span, far))
        e_send[pl.ds(index * group, group)] = rows.astype(BF16).reshape(group, held, feature)
        onward(which, lambda peer, slot: e_copy(peer, slot).start())

    def forwarded(slot, source):
        return to_other(4 + slot, source, e_other.at[slot])

    e_recv[near * group] = e_send[me]
    forwarded(near * group, e_send.at[me]).start()

    in_chunks(core * half, in_mine)
    gate = 2.0 * folded(mm(coef_rows, a_recv[...]))

    pl.when(core == 0)(drain)
    hidden_copy.wait()
    tower_three = jnp.concatenate(
        [tower_high.astype(F32), tower_low.astype(F32), tower_high.astype(F32)], axis=0
    ).astype(BF16)

    @pl.loop(0, half)
    def _(step):
        span = pl.ds(pl.multiple_of(step * chunk, chunk), chunk)
        high, low = halves(hidden_mine[step] + hidden_recv[step])
        three = jnp.concatenate([high, high, low], axis=0).astype(BF16)
        out_sum_ref[span, :] = mm(three, tower_three, 0, 0)

    in_copy.wait()

    @pl.loop(0, half)
    def _(step):
        span = pl.ds(pl.multiple_of(step * chunk, chunk), chunk)
        in_sum_ref[span, :] = in_sum_ref[span, :] + in_mine[span, :]

    for which in ("far", "near"):
        backward_from(which, 0, group, lambda peer, slot: d_copy(peer, slot, me).wait_send())
    rows_copy.wait()
    loads[11].wait()
    table_rows = table_ref.shape[0]
    part = table_rows // 4

    @pl.loop(0, 4)
    def _(step):
        numbers = (iota((part, entries), 0) + step * part).astype(F32)
        for index, row_numbers in enumerate((rows_mine, rows_other)):
            span = pl.ds(pl.multiple_of(index * table_rows + step * part, part), part)
            pre_ref[span, pl.ds(0, entries)] = jnp.where(
                numbers == row_numbers[0:1, :], STEP_SIZE, 0.0
            ).astype(BF16)

    def landed(peer, slot):
        e_copy(peer, slot).wait_recv()
        forwarded(slot, e_recv.at[slot]).start()

    def gather(index, values):
        half_entries = entries // 2
        lane_span = pl.ds(pl.multiple_of(near * half_entries, 128), half_entries)
        match = pre_ref[pl.ds(index * table_rows, table_rows), lane_span]
        sources = values[pl.ds(near * group, group)].reshape(half_entries, feature)
        table_ref[...] = table_ref[...] - mm(match, sources)

    backward_from("near", 0, group, landed)
    everyone_back(lambda peer, slot: t_copy(peer, peer).wait_recv())
    summed = t_recv[0]
    for source in range(1, count):
        summed = summed + t_recv[source]
    mine = jnp.concatenate([summed, gate[2:4], jnp.zeros((4, feature), F32)], axis=0)
    s_send[...] = mine
    small_copy = to_other(3, s_send, s_recv)
    small_copy.start()
    everyone_on(lambda peer, slot: t_copy(peer, me).wait_send())
    gather(0, e_recv)
    backward_from("far", 0, group, landed)
    everyone_on(lambda peer, slot: e_copy(peer, slot).wait_send())
    small_copy.wait()
    both = mine + s_recv[...]
    tower_sum_ref[...] = both[0:2]
    gate_sum_ref[...] = both[2:4]

    def crossed(peer, slot):
        forwarded(slot, e_recv.at[slot]).wait()

    crossed(me, near * group)
    backward_from("near", 0, group, crossed)
    gather(1, e_other)
    backward_from("far", 0, group, crossed)


def write_out(
    in_sum,
    out_sum,
    gate_sum,
    tower_sum,
    e_recv,
    e_other,
    matches,
    table_ref,
    in_out,
    out_out,
    gate_out,
    tower_out,
    table_out,
    sem,
):
    copies = []

    def start(source, target):
        copies.append(pltpu.make_async_copy(source, target, sem.at[len(copies)]))
        copies[-1].start()

    for source, target in ((in_sum, in_out), (out_sum, out_out)):
        rows = source.shape[0] // 4
        for part in range(4):
            span = pl.ds(part * rows, rows)
            start(source.at[span], target.at[span])
    start(gate_sum, gate_out)
    start(tower_sum, tower_out)
    group, held = e_recv.shape[0] // 2, e_recv.shape[1]
    half = group * held
    far = 1 - lax.div(lax.axis_index("expert"), group)
    lane_span = pl.ds(pl.multiple_of(far * half, 128), half)
    far_values = [
        values[pl.ds(far * group, group)].reshape(half, values.shape[2]) for values in (e_recv, e_other)
    ]
    table_rows = table_ref.shape[0]
    rows = table_rows // 4
    for part in range(4):
        span = pl.ds(part * rows, rows)
        total = table_ref[span, :]
        for index, values in enumerate(far_values):
            total = total - mm(matches[pl.ds(index * table_rows + part * rows, rows), lane_span], values)
        table_ref[span, :] = total
        start(table_ref.at[span], table_out.at[span])
    for copy in copies:
        copy.wait()


def on_device(
    pooled,
    routes,
    labels,
    in_weight,
    out_weight,
    gate_weight,
    tower_weight,
    tower_bias,
    bag_rows,
    bag_sample,
    bag_weight,
    row_table,
):
    count = lax.axis_size("expert")
    tok_rows, feature = pooled.shape
    tasks = tower_weight.shape[0]
    hidden = in_weight.shape[1]
    cap = -(-(3 * tok_rows // count) // 8) * 8
    rows_all = count * cap
    chunk = 1024 if rows_all * 1024 < 2**20 else 512
    chunks = hidden // chunk
    per_owner = bag_rows.shape[0] // count
    held = -(-per_owner // 8) * 8
    entries = count * held

    def bags(values, empty):
        if held == per_owner:
            return values
        return jnp.pad(
            values.reshape(count, per_owner), ((0, 0), (0, held - per_owner)), constant_values=empty
        )

    vmem = pl.BlockSpec(memory_space=pltpu.VMEM)
    anywhere = pl.BlockSpec(memory_space=pl.ANY)
    routed = (rows_all, feature)
    owned = (count, held, feature)
    half_rows = hidden // 2
    halved = (chunks // 2, 8, chunk)
    in_hbm = [
        pltpu.with_memory_space_constraint(value, pltpu.HBM)
        for value in (
            pooled,
            routes.T,
            labels.T,
            in_weight[0],
            out_weight[0],
            gate_weight,
            tower_weight,
            tower_bias,
            bag_rows.reshape(-1, 128),
            bags(bag_sample, -1).reshape(1, -1),
            bags(bag_weight, 0.0).reshape(1, -1),
            row_table,
        )
    ]
    results = pl.pallas_call(
        functools.partial(kernel, (count, cap, chunk, chunks, per_owner)),
        out_shape=(
            pltpu.VMEM((half_rows, feature), F32),
            pltpu.VMEM((half_rows, feature), F32),
            pltpu.VMEM((tasks, feature), F32),
            pltpu.VMEM((tasks, feature), F32),
            pltpu.VMEM(owned, BF16),
            pltpu.VMEM(owned, BF16),
            pltpu.VMEM((hidden, rows_all), BF16),
            pltpu.VMEM(row_table.shape, F32),
        ),
        in_specs=[anywhere] * 12,
        out_specs=(vmem,) * 8,
        scratch_shapes=[
            pltpu.VMEM(pooled.shape, BF16),
            pltpu.VMEM((2, tok_rows), jnp.int32),
            pltpu.VMEM((2, tok_rows), jnp.int32),
            pltpu.VMEM(gate_weight.shape, BF16),
            pltpu.VMEM(tower_weight.shape, F32),
            pltpu.SMEM(tower_bias.shape, F32),
            pltpu.VMEM((bag_rows.shape[0] // 128, 128), jnp.int32),
            pltpu.VMEM((1, entries), jnp.int32),
            pltpu.VMEM((1, entries), F32),
            pltpu.VMEM((hidden, feature), BF16),
            pltpu.VMEM((hidden, feature), BF16),
            pltpu.VMEM((chunks, feature, chunk), BF16),
            pltpu.VMEM((chunks, 16, chunk), BF16),
            pltpu.VMEM((2, hidden, 128), F32),
            pltpu.VMEM((hidden, rows_all), BF16),
            pltpu.VMEM((hidden, rows_all), F32),
            pltpu.VMEM((entries, rows_all), BF16),
            pltpu.VMEM((entries, feature), F32),
            pltpu.VMEM((entries, 128), F32),
            pltpu.VMEM(routed, BF16),
            pltpu.VMEM(routed, BF16),
            pltpu.VMEM((count, 2, 128), F32),
            pltpu.VMEM((count, 2, 128), F32),
            pltpu.VMEM((2, 8, 128), F32),
            pltpu.VMEM((count, 2, 8, 128), F32),
            pltpu.VMEM(routed, BF16),
            pltpu.VMEM(routed, BF16),
            pltpu.VMEM(owned, BF16),
            pltpu.VMEM((2, feature), F32),
            pltpu.VMEM((count, 2, feature), F32),
            pltpu.VMEM((8, feature), F32),
            pltpu.VMEM((8, feature), F32),
            pltpu.VMEM((8, entries), F32),
            pltpu.VMEM((8, entries), F32),
            pltpu.VMEM(halved, F32),
            pltpu.VMEM(halved, F32),
            pltpu.VMEM(halved, F32),
            pltpu.VMEM((16, rows_all), F32),
            pltpu.VMEM((feature, rows_all), F32),
            pltpu.SemaphoreType.DMA((7, count)),
            pltpu.SemaphoreType.DMA((7, count)),
            pltpu.SemaphoreType.DMA((4 + count,)),
            pltpu.SemaphoreType.DMA((4 + count,)),
            pltpu.SemaphoreType.DMA((12,)),
        ],
        compiler_params=pltpu.CompilerParams(
            collective_id=0, has_side_effects=True, vmem_limit_bytes=VMEM_LIMIT
        ),
    )(*in_hbm)
    in_grad, out_grad, gate_grad, tower_grad, table = pl.pallas_call(
        write_out,
        out_shape=[jax.ShapeDtypeStruct(value.shape, F32) for value in results[:4]]
        + [jax.ShapeDtypeStruct(row_table.shape, F32)],
        in_specs=[vmem] * 8,
        out_specs=[anywhere] * 5,
        scratch_shapes=[pltpu.SemaphoreType.DMA((16,))],
        compiler_params=pltpu.CompilerParams(vmem_limit_bytes=4 * 2**20),
    )(*[pltpu.with_memory_space_constraint(value, pltpu.VMEM) for value in results])
    return (in_grad[None], out_grad[None], gate_grad[None], tower_grad, table)


def solution(mesh):
    in_specs = (
        P(("expert", "dp"), None),
        P(("expert", "dp"), None),
        P(("expert", "dp"), None),
        P("expert", None, None),
        P("expert", None, None),
        P(),
        P(),
        P(),
        P(("expert", "dp")),
        P(("expert", "dp")),
        P(("expert", "dp")),
        P("expert", None),
    )
    out_specs = (
        P("expert", "dp", None),
        P("expert", "dp", None),
        P("expert", None, None),
        P(),
        P("expert", None),
    )
    return jax.shard_map(
        on_device, mesh=mesh, in_specs=in_specs, out_specs=out_specs, check_vma=False
    )
```
